32 devices in a mesh: gx: 4 (over z), gy: 2 (over y), gz: 4 (over x, core).
Axes of the slice: x: 2, y: 2, z: 4, core: 2. Of those that a mesh axis runs over, the one named last changes fastest.
Arguments:
- positions: float32 [8, 4, 8, 3, 128], P('gx', 'gy', 'gz'), may hold values from 0 to 64, as said below
- velocities: float32 [8, 4, 8, 3, 128], P('gx', 'gy', 'gz'), may hold values from -5 to 5
- species: int32 [8, 4, 8, 128], P('gx', 'gy', 'gz'), may hold values from 0 to 3, as said below
- neighbour_blocks: int32 [8, 4, 8, 8], P('gx', 'gy', 'gz'), may hold values from 0 to 27, as said below
- embedding: bfloat16 [4, 64], replicated, may hold values from -6 to 6
- w_send: bfloat16 [2, 64, 64], replicated, may hold values from -0.75 to 0.75
- w_radial: float32 [2, 8, 64], replicated, may hold values from -4 to 4
- w_update: bfloat16 [2, 64, 64], replicated, may hold values from -0.75 to 0.75
- w_out: bfloat16 [64, 64], replicated, may hold values from -0.75 to 0.75
- w_energy: float32 [64], replicated, may hold values from -5 to 5
- masses: float32 [4], replicated, may hold values from 0.5 to 8
Outputs:
- displacement: float32 [8, 4, 8, 3, 128], P('gx', 'gy', 'gz')
- new_velocity: float32 [8, 4, 8, 3, 128], P('gx', 'gy', 'gz')
The draws below stay inside these ranges and needn't reach their ends.
Inputs may be any that keep to these rules, and one draw needn't show every extreme that they name: `positions`: each atom slot lies in the cube of side 8 whose lowest corner is 8 times its block's coordinates. `species`: 0 marks an empty slot; in each block the empty slots follow the occupied ones, and at least 32 slots are occupied. `neighbour_blocks`: entry o below 27 is the offset 9 (dx + 1) + 3 (dy + 1) + (dz + 1) of a source block; 27 marks an empty slot. The first entry is 13, the block itself; live entries of a block are distinct and come before its empty slots; each block has two or more live entries.
All inputs are finite; a program needn't handle non-finite values.
Results may differ from the reference program's by a relative error of at most 0.039.
Values may be sent and summed in bfloat16 or wider, within the bound.
A program may use at most 64 MiB of HBM per device.

```python
import math
import jax
import jax.numpy as jnp
from jax import lax

C = 64
K = 8
SPECIES = 4
A = 128
NT = 8
STEPS = 1
NBX = 8
NBY = 4
NBZ = 8


block_side = 8.0


def draw_positions(key, part):
    full_shape = (NBX, NBY, NBZ, 3, A)
    component = lax.broadcasted_iota(jnp.int32, full_shape, 3)
    index_x = lax.broadcasted_iota(jnp.float32, full_shape, 0)
    index_y = lax.broadcasted_iota(jnp.float32, full_shape, 1)
    index_z = lax.broadcasted_iota(jnp.float32, full_shape, 2)
    anchor = jnp.where(component == 0, index_x, jnp.where(component == 1, index_y, index_z)) * block_side
    unit_draw = jax.random.uniform(jax.random.fold_in(key, 11), full_shape, jnp.float32)
    return anchor + block_side * unit_draw


def draw_velocities(key, part):
    full_shape = (NBX, NBY, NBZ, 3, A)
    frac_x = lax.broadcasted_iota(jnp.float32, full_shape, 0) / (NBX - 1)
    frac_y = lax.broadcasted_iota(jnp.float32, full_shape, 1) / (NBY - 1)
    frac_z = lax.broadcasted_iota(jnp.float32, full_shape, 2) / (NBZ - 1)
    spread = 0.15 * jnp.exp(0.5 * jnp.log(3.0) * (frac_x + frac_y + frac_z))
    base = jnp.clip(jax.random.normal(jax.random.fold_in(key, 42), full_shape, jnp.float32), -6.0, 6.0)
    return base * spread


def draw_species(key, part):
    key_fill = jax.random.fold_in(key, 21)
    key_kind = jax.random.fold_in(key, 22)
    filled = jax.random.randint(key_fill, (NBX, NBY, NBZ, 1), A // 4, A + 1)
    species_draw = jax.random.randint(key_kind, (NBX, NBY, NBZ, A), 1, SPECIES)
    slot_index = lax.broadcasted_iota(jnp.int32, (NBX, NBY, NBZ, A), 3)
    return jnp.where(slot_index < filled, species_draw, 0).astype(jnp.int32)


def draw_neighbour_blocks(key, part):
    key_rank = jax.random.fold_in(key, 31)
    key_count = jax.random.fold_in(key, 32)
    scores = jax.random.randint(key_rank, (NBX, NBY, NBZ, 26), 0, 1 << 20) * 32
    scores = scores + lax.broadcasted_iota(jnp.int32, (NBX, NBY, NBZ, 26), 3)
    ranking = jnp.argsort(scores, axis=-1, stable=True).astype(jnp.int32)
    others = ranking + (ranking >= 13).astype(jnp.int32)
    listing = jnp.concatenate([jnp.full((NBX, NBY, NBZ, 1), 13, jnp.int32), others[..., :NT - 1]], axis=-1)
    live_count = jax.random.randint(key_count, (NBX, NBY, NBZ, 1), 2, NT + 1)
    slot_index = lax.broadcasted_iota(jnp.int32, (NBX, NBY, NBZ, NT), 3)
    return jnp.where(slot_index < live_count, listing, 27).astype(jnp.int32)


def bell_draw(stream_key, extent, width, reach, kind=jnp.bfloat16):
    return jnp.clip(width * jax.random.normal(stream_key, extent, jnp.float32), -reach, reach).astype(kind)


def setup_inputs(seed: int = 0) -> dict:
    splits = jax.random.split(jax.random.key(seed), 12)
    positions = draw_positions(jax.random.fold_in(splits[11], 71), 0)
    velocities = draw_velocities(jax.random.fold_in(splits[11], 71), 0)
    species = draw_species(jax.random.fold_in(splits[11], 71), 0)
    neighbour_blocks = draw_neighbour_blocks(jax.random.fold_in(splits[11], 71), 0)
    embedding = bell_draw(splits[4], (SPECIES, C), 1.0, 6.0)
    w_send = bell_draw(splits[5], (2, C, C), C ** -0.5, 0.75)
    w_radial = bell_draw(splits[6], (2, K, C), 0.3, 4.0, jnp.float32)
    w_update = bell_draw(splits[7], (2, C, C), C ** -0.5, 0.75)
    w_out = bell_draw(splits[8], (C, C), C ** -0.5, 0.75)
    w_energy = bell_draw(splits[9], (C,), 0.35, 5.0, jnp.float32)
    masses = jnp.clip(jnp.exp(jax.random.uniform(splits[10], (SPECIES,), jnp.float32, math.log(0.5), math.log(8.0))), 0.5, 8.0)
    return {"positions": positions, "velocities": velocities, "species": species, "neighbour_blocks": neighbour_blocks, "embedding": embedding, "w_send": w_send, "w_radial": w_radial, "w_update": w_update, "w_out": w_out, "w_energy": w_energy, "masses": masses}


soft_sq = 0.25
cut_sq = 25.0
gamma_width = 2.56
time_step = 1.0
target_slot = 0.25
tiny_eps = 1e-06

def slot_tables(neighbour_blocks):
    size_x, size_y, size_z, slot_count = neighbour_blocks.shape
    is_live = neighbour_blocks < 27
    offset = jnp.where(is_live, neighbour_blocks, 13)
    step_x = offset // 9 - 1
    step_y = offset // 3 % 3 - 1
    step_z = offset % 3 - 1
    index_x = lax.broadcasted_iota(jnp.int32, neighbour_blocks.shape, 0)
    index_y = lax.broadcasted_iota(jnp.int32, neighbour_blocks.shape, 1)
    index_z = lax.broadcasted_iota(jnp.int32, neighbour_blocks.shape, 2)
    source = ((index_x + 1 + step_x) * (size_y + 2) + (index_y + 1 + step_y)) * (size_z + 2) + (index_z + 1 + step_z)
    target = ((index_x[..., 0] + 1) * (size_y + 2) + index_y[..., 0] + 1) * (size_z + 2) + index_z[..., 0] + 1
    return (source.reshape(-1, slot_count).astype(jnp.int32), target.reshape(-1).astype(jnp.int32), is_live.astype(jnp.float32).reshape(-1, slot_count), (neighbour_blocks == 13).astype(jnp.float32).reshape(-1, slot_count))

def feature_table(species_ext, embedding):
    kind_count = embedding.shape[0]
    onehot = (species_ext[..., None, :] == lax.broadcasted_iota(jnp.int32, (kind_count, 1), 0)).astype(jnp.float32)
    return jnp.einsum('sc,...sa->...ca', embedding.astype(jnp.float32), onehot)

def inverse_mass(species, masses):
    kind_count = masses.shape[0]
    onehot = (species[..., None, :] == lax.broadcasted_iota(jnp.int32, (kind_count, 1), 0)).astype(jnp.float32)
    return 1.0 / jnp.einsum('s,...sa->...a', masses, onehot)[..., None, :]

def pair_kernel(target_pos, target_real, source_pos, source_real, slot_live, slot_self, basis_count):
    offset = source_pos[:, :, None, :] - target_pos[None, :, :, None]
    squared = lax.optimization_barrier(jnp.sum(offset * offset, axis=1))
    distance = jnp.sqrt(squared + soft_sq)
    cutoff = jnp.square(jax.nn.relu(1.0 - squared / cut_sq))
    atom_count = target_pos.shape[-1]
    diagonal = (lax.broadcasted_iota(jnp.int32, (atom_count, atom_count), 0) == lax.broadcasted_iota(jnp.int32, (atom_count, atom_count), 1)).astype(jnp.float32)
    weight = cutoff * target_real[None, :, None] * source_real[:, None, :] * slot_live[:, None, None]
    weight = weight * (1.0 - slot_self[:, None, None] * diagonal[None])
    centers = (lax.iota(jnp.float32, basis_count) + 0.5) * (5.0 / basis_count)
    radial = jnp.exp(-gamma_width * jnp.square(distance[None] - centers[:, None, None, None]))
    return (weight[None] * radial).astype(jnp.bfloat16)

def block_message(kernel, source_feat, w_send, w_radial):
    sender = jnp.einsum('qcj,cd->qdj', source_feat.astype(jnp.bfloat16).astype(jnp.float32), w_send.astype(jnp.float32)).astype(jnp.bfloat16)
    partial_value = jnp.einsum('kqij,qdj->kdi', kernel.astype(jnp.float32), sender.astype(jnp.float32))
    return lax.optimization_barrier(jnp.sum(partial_value * w_radial[:, :, None], axis=0)).astype(jnp.bfloat16)

def block_update(target_feat, message, w_update):
    update = jnp.einsum('ci,cd->di', message.astype(jnp.float32), w_update.astype(jnp.float32))
    return target_feat + jax.nn.silu(update)

def layer_one(flat_pos, flat_feat, flat_real, tables, w_send, w_radial, w_update):

    def one_block(entry):
        source_idx, target_idx, slot_live, slot_self = entry
        kernel = pair_kernel(flat_pos[target_idx], flat_real[target_idx], jnp.take(flat_pos, source_idx, axis=0), jnp.take(flat_real, source_idx, axis=0), slot_live, slot_self, w_radial.shape[1])
        message = block_message(kernel, jnp.take(flat_feat, source_idx, axis=0), w_send[0], w_radial[0])
        return block_update(flat_feat[target_idx], message, w_update[0])
    layer_out = lax.map(jax.checkpoint(one_block), tables)
    return lax.optimization_barrier(layer_out.astype(jnp.bfloat16)).astype(jnp.float32)

def layer_two_energy(flat_pos, flat_feat, flat_real, tables, w_send, w_radial, w_update, w_out, w_energy):

    def one_block(entry):
        source_idx, target_idx, slot_live, slot_self = entry
        target_real = flat_real[target_idx]
        kernel = pair_kernel(flat_pos[target_idx], target_real, jnp.take(flat_pos, source_idx, axis=0), jnp.take(flat_real, source_idx, axis=0), slot_live, slot_self, w_radial.shape[1])
        message = block_message(kernel, jnp.take(flat_feat, source_idx, axis=0), w_send[1], w_radial[1])
        second = block_update(flat_feat[target_idx], message, w_update[1])
        hidden = jnp.einsum('ci,cd->di', second.astype(jnp.bfloat16).astype(jnp.float32), w_out.astype(jnp.float32))
        per_atom = lax.optimization_barrier(jnp.sum(jax.nn.silu(hidden) * w_energy[:, None], axis=0)) * target_real
        return jnp.sum(per_atom)
    return jnp.sum(lax.map(jax.checkpoint(one_block), tables))

def reference(positions, velocities, species, neighbour_blocks, embedding, w_send, w_radial, w_update, w_out, w_energy, masses):
    grid_x, grid_y, grid_z = (positions.shape[0], positions.shape[1], positions.shape[2])
    atom_count = positions.shape[-1]
    channels = w_send.shape[-1]
    species_ext = jnp.pad(species, ((1, 1), (1, 1), (1, 1), (0, 0)))
    flat_feat = feature_table(species_ext, embedding).reshape(-1, channels, atom_count)
    flat_real = (species_ext > 0).astype(jnp.float32).reshape(-1, atom_count)
    tables = slot_tables(neighbour_blocks)
    inverse = inverse_mass(species, masses)
    padding = ((1, 1), (1, 1), (1, 1), (0, 0), (0, 0))

    def total_energy(coords):
        flat_pos = jnp.pad(coords, padding).reshape(-1, 3, atom_count)
        layer_out = layer_one(flat_pos, flat_feat, flat_real, tables, w_send, w_radial, w_update)
        grid_feat = layer_out.reshape(grid_x, grid_y, grid_z, channels, atom_count)
        flat_hidden = jnp.pad(grid_feat, padding).reshape(-1, channels, atom_count)
        return layer_two_energy(flat_pos, flat_hidden, flat_real, tables, w_send, w_radial, w_update, w_out, w_energy)

    def forces(coords):
        return -jax.grad(total_energy)(coords)
    coords = positions
    velocity = velocities
    travelled = jnp.zeros_like(positions)
    force_now = forces(coords)
    for stepno in range(STEPS):
        half_kick = velocity + 0.5 * time_step * force_now * inverse
        coords = coords + time_step * half_kick
        travelled = travelled + time_step * half_kick
        force_now = forces(coords)
        velocity = half_kick + 0.5 * time_step * force_now * inverse
    real_here = (species > 0).astype(jnp.float32)[..., None, :]
    kinetic = jnp.sum(real_here * 0.5 / inverse * velocity * velocity)
    slot_total = positions.size // 3
    factor = jnp.sqrt(target_slot * slot_total / (kinetic + tiny_eps))
    return (travelled, velocity * factor)
```

```python
import functools
import math

import jax
import jax.numpy as jnp
from jax import lax
from jax.experimental import pallas as pl
from jax.experimental.pallas import tpu as pltpu
from jax.sharding import PartitionSpec as P

soft_sq = 0.25
cut_sq = 25.0
gamma_width = 2.56
time_step = 1.0
target_slot = 0.25
tiny_eps = 1e-06
LOG2E = math.log2(math.e)
CHUNK = 32
bf16 = jnp.bfloat16
f32 = jnp.float32

SIDES = (("gx", 0), ("gy", 1), ("gz", 2))


MESH = pl.DeviceIdType.MESH


DIRECTIONS = [
    (dx, dy, dz) for dx in (-1, 0, 1) for dy in (-1, 0, 1) for dz in (-1, 0, 1) if dx or dy or dz
]


def around(direction):
    present, place = True, {}
    for (axis, _), step in zip(SIDES, direction):
        if step:
            there = lax.axis_index(axis) + step
            present = present & (there >= 0) & (there < lax.axis_size(axis))
            place[axis] = there
    return present, place


def opposite(direction):
    return tuple(-step for step in direction)


def greet(more=()):
    barrier = pltpu.get_barrier_semaphore()
    expected = len(more)
    for place in more:
        pl.semaphore_signal(barrier, inc=1, device_id=place, device_id_type=MESH)
    for direction in DIRECTIONS:
        present, place = around(direction)

        @pl.when(present)
        def _(place=place):
            pl.semaphore_signal(barrier, inc=1, device_id=place, device_id_type=MESH)

        expected = expected + present.astype(jnp.int32)
    pl.semaphore_wait(barrier, expected)


def sent(direction, sizes):
    own, ext = [], []
    for step, size in zip(direction, sizes):
        own.append(pl.ds(0, size) if step == 0 else pl.ds(0 if step < 0 else size - 1, 1))
        ext.append(pl.ds(1, size) if step == 0 else pl.ds(size + 1 if step < 0 else 0, 1))
    return tuple(own), tuple(ext)


def rim(direction, sizes):
    return tuple(
        pl.ds(1, size) if step == 0 else pl.ds(0 if step < 0 else size + 1, 1)
        for step, size in zip(direction, sizes)
    )


def exchange(pairs, send_sem, recv_sem):
    copies = []
    for at, (direction, (source, target)) in enumerate(zip(DIRECTIONS, pairs)):
        present, place = around(direction)
        copy = pltpu.make_async_remote_copy(
            src_ref=source,
            dst_ref=target,
            send_sem=send_sem.at[at],
            recv_sem=recv_sem.at[at],
            device_id=place,
            device_id_type=MESH,
        )
        pl.when(present)(copy.start)
        copies.append((copy, present, around(opposite(direction))[0]))

    def finish():
        for copy, _, arrives in copies:
            pl.when(arrives)(copy.wait_recv)
        for copy, present, _ in copies:
            pl.when(present)(copy.wait_send)

    return finish


def blank_rim(ext, sizes):
    for direction in DIRECTIONS:

        @pl.when(jnp.logical_not(around(direction)[0]))
        def _(direction=direction):
            index = rim(direction, sizes)
            ext[index] = jnp.zeros(tuple(part.size for part in index) + ext.shape[3:], ext.dtype)


def spread_rim(own, ext, sizes, send_sem, recv_sem):
    pairs = []
    for direction in DIRECTIONS:
        mine, theirs = sent(direction, sizes)
        pairs.append((own.at[mine], ext.at[theirs]))
    return exchange(pairs, send_sem, recv_sem)


def halo_kernel(own, ext, send_sem, recv_sem, copy_sem):
    sizes = own.shape[:3]
    fill = pltpu.make_async_copy(own, ext.at[tuple(pl.ds(1, size) for size in sizes)], copy_sem)
    fill.start()
    blank_rim(ext, sizes)
    greet()
    finish = spread_rim(own, ext, sizes, send_sem, recv_sem)
    fill.wait()
    finish()


def landing_scratch(sizes, tail, dtype):
    return [
        pltpu.VMEM(tuple(1 if step else size for step, size in zip(direction, sizes)) + tail, dtype)
        for direction in DIRECTIONS
    ]


def blank_lands(lands):
    for direction, land in zip(DIRECTIONS, lands):

        @pl.when(jnp.logical_not(around(opposite(direction))[0]))
        def _(land=land):
            land[...] = jnp.zeros_like(land)


def gather_rim(ext, lands, sizes, send_sem, recv_sem):
    pairs = [(ext.at[rim(direction, sizes)], land) for direction, land in zip(DIRECTIONS, lands)]
    return exchange(pairs, send_sem, recv_sem)


def cells_of(sizes):
    return [(x, y, z) for x in range(sizes[0]) for y in range(sizes[1]) for z in range(sizes[2])]


def landed(ext, lands, sizes, cell):
    value = ext[tuple(at + 1 for at in cell)].astype(f32)
    for direction, land in zip(DIRECTIONS, lands):
        index = []
        for step, size, at in zip(direction, sizes, cell):
            if step == 0:
                index.append(at)
            elif at == (size - 1 if step < 0 else 0):
                index.append(0)
        if len(index) == 3:
            value = value + land[tuple(index)].astype(f32)
    return value


def fold_kernel(ext, own, *refs):
    lands, (send_sem, recv_sem) = refs[:26], refs[26:]
    sizes = own.shape[:3]
    blank_lands(lands)
    greet()
    gather_rim(ext, lands, sizes, send_sem, recv_sem)()
    for cell in cells_of(sizes):
        own[cell] = landed(ext, lands, sizes, cell).astype(own.dtype)


def kick_kernel(ext, start, half, inverse, out_half, out_moved, out_pos, *refs):
    lands, (send_sem, recv_sem, send_two, recv_two, copy_sem, fresh) = refs[:26], refs[26:]
    sizes = start.shape[:3]
    blank_lands(lands)
    blank_rim(out_pos, sizes)
    greet()
    gather_rim(ext, lands, sizes, send_sem, recv_sem)()
    row = lax.broadcasted_iota(jnp.int32, start.shape[3:], 0)
    for cell in cells_of(sizes):
        force = -landed(ext, lands, sizes, cell)
        half_kick = half[cell] + 0.5 * time_step * force * inverse[cell]
        moved = time_step * half_kick
        out_half[cell] = half_kick
        out_moved[cell] = moved[:3]
        fresh[cell] = start[cell] + jnp.where(row < 3, moved, 0.0)
    fill = pltpu.make_async_copy(fresh, out_pos.at[tuple(pl.ds(1, size) for size in sizes)], copy_sem)
    fill.start()
    finish = spread_rim(fresh, out_pos, sizes, send_two, recv_two)
    fill.wait()
    finish()


def ring(axes):
    steps = [()]
    for axis in axes:
        steps = [step + (t,) for step in steps for t in range(lax.axis_size(axis))]
    places = []
    for step in steps[1:]:
        places.append(
            {axis: lax.rem(lax.axis_index(axis) + t, lax.axis_size(axis)) for axis, t in zip(axes, step) if t}
        )
    return places


STAGES = (("gx", "gy"), ("gz",))


def last_kernel(slot_total, ext, half, inverse, weight, out, *refs):
    lands, refs = refs[:26], refs[26:]
    send_sem, recv_sem, send_two, recv_two, speed = refs[:5]
    inbox, sums = refs[5:7], refs[7:9]
    sizes = half.shape[:3]
    blank_lands(lands)
    greet([place for axes in STAGES for place in ring(axes)])
    gather_rim(ext, lands, sizes, send_sem, recv_sem)()
    row = lax.broadcasted_iota(jnp.int32, half.shape[3:], 0)
    total = jnp.zeros(half.shape[3:], f32)
    for cell in cells_of(sizes):
        force = -landed(ext, lands, sizes, cell)
        velocity = half[cell] + 0.5 * time_step * force * inverse[cell]
        speed[cell] = velocity
        total = total + jnp.where(row < 3, 0.5 * weight[cell] * velocity * velocity, 0.0)
    base = 0
    for stage, axes in enumerate(STAGES):
        sums[stage][...] = total
        copies = []
        for t, place in enumerate(ring(axes)):
            copy = pltpu.make_async_remote_copy(
                src_ref=sums[stage],
                dst_ref=inbox[stage].at[t],
                send_sem=send_two.at[base],
                recv_sem=recv_two.at[base],
                device_id=place,
                device_id_type=MESH,
            )
            copy.start()
            copies.append(copy)
            base += 1
        for t, copy in enumerate(copies):
            copy.wait()
            total = total + inbox[stage][t]
    kinetic = jnp.sum(total, keepdims=True)
    factor = jnp.sqrt(target_slot * slot_total / (kinetic + tiny_eps))
    for cell in cells_of(sizes):
        out[cell] = (speed[cell] * factor)[:3]


def vmem_specs(count):
    return [pl.BlockSpec(memory_space=pltpu.VMEM)] * count


def remote_call(kernel, outs, scratch, collective_id, args):
    return pl.pallas_call(
        kernel,
        out_shape=outs,
        in_specs=vmem_specs(len(args)),
        out_specs=vmem_specs(len(outs)),
        scratch_shapes=scratch,
        compiler_params=pltpu.CompilerParams(
            collective_id=collective_id, has_side_effects=True, vmem_limit_bytes=16 << 20
        ),
    )(*args)


def semaphores():
    return [pltpu.SemaphoreType.DMA((26,)), pltpu.SemaphoreType.DMA((26,))]


def padded_shape(cells):
    return jax.ShapeDtypeStruct(tuple(size + 2 for size in cells.shape[:3]) + cells.shape[3:], cells.dtype)


def padded(cells, collective_id):
    scratch = semaphores() + [pltpu.SemaphoreType.DMA]
    return remote_call(halo_kernel, [padded_shape(cells)], scratch, collective_id, (cells,))[0]


def folded(grid, sizes, collective_id):
    tail = grid.shape[3:]
    scratch = landing_scratch(sizes, tail, grid.dtype) + semaphores()
    out = jax.ShapeDtypeStruct(sizes + tail, grid.dtype)
    return remote_call(fold_kernel, [out], scratch, collective_id, (grid,))[0]


def kicked(grid, start, half, inverse, collective_id):
    sizes, tail = start.shape[:3], start.shape[3:]
    scratch = landing_scratch(sizes, tail, f32) + semaphores() + semaphores()
    scratch += [pltpu.SemaphoreType.DMA, pltpu.VMEM(start.shape, f32)]
    moved = jax.ShapeDtypeStruct(sizes + (3,) + tail[1:], f32)
    outs = [jax.ShapeDtypeStruct(start.shape, f32), moved, padded_shape(start)]
    return remote_call(kick_kernel, outs, scratch, collective_id, (grid, start, half, inverse))


def thermostat(grid, half, inverse, weight, slot_total, collective_id):
    sizes, tail = half.shape[:3], half.shape[3:]
    counts = [math.prod(lax.axis_size(axis) for axis in axes) for axes in STAGES]
    peers = sum(count - 1 for count in counts)
    scratch = landing_scratch(sizes, tail, f32) + semaphores()
    scratch += [pltpu.SemaphoreType.DMA((peers,)), pltpu.SemaphoreType.DMA((peers,)), pltpu.VMEM(half.shape, f32)]
    scratch += [pltpu.VMEM((max(count - 1, 1),) + tail, f32) for count in counts]
    scratch += [pltpu.VMEM(tail, f32)] * 2
    out = jax.ShapeDtypeStruct(sizes + (3,) + tail[1:], f32)
    kernel = functools.partial(last_kernel, float(slot_total))
    return remote_call(kernel, [out], scratch, collective_id, (grid, half, inverse, weight))[0]


def slot_tables(neighbour_blocks):
    size_x, size_y, size_z, slot_count = neighbour_blocks.shape
    is_live = neighbour_blocks < 27
    offset = jnp.where(is_live, neighbour_blocks, 13)
    index_x = lax.broadcasted_iota(jnp.int32, neighbour_blocks.shape, 0)
    index_y = lax.broadcasted_iota(jnp.int32, neighbour_blocks.shape, 1)
    index_z = lax.broadcasted_iota(jnp.int32, neighbour_blocks.shape, 2)
    source = (
        (index_x + offset // 9) * (size_y + 2) + (index_y + offset // 3 % 3)
    ) * (size_z + 2) + (index_z + offset % 3)
    live = jnp.sum(is_live.astype(jnp.int32), axis=-1)
    return source.reshape(-1, slot_count), live.reshape(-1)


def basis_constants(basis_count):
    step = 5.0 / basis_count
    mid = basis_count // 2
    centers = [(k + 0.5) * step for k in range(basis_count)]
    scales = [math.exp(-gamma_width * (centers[k] - centers[mid]) ** 2) for k in range(basis_count)]
    return step, mid, centers, scales


def geometry(apart, row0, basis_count):
    step, mid, centers, _ = basis_constants(basis_count)
    atoms = apart.shape[1] // 3
    rows = slice(row0, row0 + CHUNK)
    steps = [apart[rows, d * atoms : (d + 1) * atoms] for d in range(3)]
    dx, dy, dz = steps
    squared = jnp.minimum(dx * dx + dy * dy + dz * dz, cut_sq)
    cut = 1.0 - squared * (1.0 / cut_sq)
    soft = squared + soft_sq
    inv = lax.rsqrt(soft)
    shift = soft * inv - centers[mid]
    bell = jnp.exp2((-gamma_width * LOG2E) * (shift * shift))
    slope = shift * (2.0 * gamma_width * step * LOG2E)
    return steps, cut, inv, bell, jnp.exp2(slope), jnp.exp2(-slope)


def radial_powers(start, up, down, basis_count):
    mid = basis_count // 2
    powers = [None] * basis_count
    powers[mid] = start
    for k in range(mid + 1, basis_count):
        powers[k] = powers[k - 1] * up
    for k in range(mid - 1, -1, -1):
        powers[k] = powers[k + 1] * down
    scales = basis_constants(basis_count)[3]
    return [power * scale if scale != 1.0 else power for power, scale in zip(powers, scales)]


def fill_kernel(store, apart, c, basis_count):
    atoms = apart.shape[0]
    for row0 in range(0, atoms, CHUNK):
        _, cut, _, bell, up, down = geometry(apart, row0, basis_count)
        ahead = lax.broadcasted_iota(jnp.int32, cut.shape, 1) - lax.broadcasted_iota(jnp.int32, cut.shape, 0)
        cut = jnp.where(ahead == row0 + c * atoms, 0.0, cut)
        for k, value in enumerate(radial_powers(cut * cut * bell, up, down, basis_count)):
            store[row0 : row0 + CHUNK, k * atoms : (k + 1) * atoms] = value.astype(bf16)


def split(value):
    high = value.astype(bf16)
    return high, (value - high.astype(f32)).astype(bf16)


def dot_split(a, value):
    high, low = split(value)
    return dot(a, high) + dot(a, low)


def held(value):
    return value.astype(bf16).astype(f32)


def narrowed(radial, sums):
    atoms = radial[0].shape[-1]
    return sum(column * sums[:, k * atoms : (k + 1) * atoms] for k, column in enumerate(radial))


def silu_grad(value):
    gate = jax.nn.sigmoid(value)
    return gate * (1.0 + value * (1.0 - gate))


def dot(a, b):
    return jnp.dot(a, b, preferred_element_type=f32)


def dot_wide(a, b):
    return jnp.dot(a, b, preferred_element_type=f32, precision=lax.Precision.HIGHEST)


def dot_nt(a, b):
    return lax.dot_general(a, b, (((1,), (1,)), ((), ())), preferred_element_type=f32)


def dot_tn(a, b):
    return lax.dot_general(a, b, (((0,), (0,)), ((), ())), preferred_element_type=f32)


FEATS = 32


def thirds(value):
    high = held(value)
    rest = value - high
    mid = held(rest)
    return high, mid, rest - mid


def side(values):
    return jnp.concatenate(values, axis=1)


def features(block, origin):
    row = lax.broadcasted_iota(jnp.int32, block.shape, 0)
    where = jnp.where(row < 3, block - origin, 0.0)
    parts = thirds(where)
    tiles = [jnp.where(row < 3, part, jnp.where(row == 3, 1.0, 0.0)) for part in parts]
    kinds = jnp.where((row > 3) & (block[3:4, :] == row.astype(f32) - 4.0), 1.0, 0.0)
    tiles[0] = jnp.where(row > 3, kinds, tiles[0])
    return jnp.concatenate(tiles + [kinds], axis=0).astype(bf16)


def set_apart(rel, own, origin):
    atoms = own.shape[-1]
    row = lax.broadcasted_iota(jnp.int32, (FEATS, atoms), 0)
    high, mid, low = thirds(own - origin)
    for d in range(3):
        tile = jnp.where((row == d) | (row == 8 + d) | (row == 16 + d), 1.0, 0.0)
        for at, part in ((3, high), (11, mid), (19, low)):
            tile = jnp.where(row == at, -part[d : d + 1, :], tile)
        rel[:, d * atoms : (d + 1) * atoms] = tile.astype(bf16)


def list_kernel(src, live, home, pos, dest, count, table, rel, hits):
    blocks, slots = src.shape
    atoms = pos.shape[-1]
    row = lax.broadcasted_iota(jnp.int32, (8, atoms), 0)
    origin = pos[home[0]][:, 0:1]
    for b in range(blocks):
        own = pos[home[b]]
        set_apart(rel.at[b], own, origin)
        real = own[3:4, :] > 0.0
        low = jnp.min(jnp.where(real, own, 1e30), axis=1, keepdims=True)
        high = jnp.max(jnp.where(real, own, -1e30), axis=1, keepdims=True)
        for q in range(slots):
            block = pos[src[b, q]]
            table[b, :, q * atoms : (q + 1) * atoms] = features(block, origin)
            gap = jnp.maximum(jnp.maximum(low - block, block - high), 0.0)
            gap = jnp.sum(jnp.where(row < 3, gap * gap, 0.0), axis=0, keepdims=True)
            near = jnp.where((gap < cut_sq * 1.001) & (block[3:4, :] > 0.0), 1.0, 0.0)
            hits[b * slots + q : b * slots + q + 1, :] = near * (q < live[b]).astype(f32)
    hit = hits[...]
    shape = (atoms, atoms)
    upto = lax.broadcasted_iota(jnp.int32, shape, 0) <= lax.broadcasted_iota(jnp.int32, shape, 1)
    inside = dot(hit.astype(bf16), jnp.where(upto, 1.0, 0.0).astype(bf16))
    total = jnp.broadcast_to(inside[:, atoms - 1 : atoms], hit.shape)
    pairs = blocks * slots
    r0 = lax.broadcasted_iota(jnp.int32, (pairs, pairs), 0)
    r1 = lax.broadcasted_iota(jnp.int32, (pairs, pairs), 1)
    group0 = jnp.floor((r0.astype(f32) + 0.5) * (1.0 / slots))
    group1 = jnp.floor((r1.astype(f32) + 0.5) * (1.0 / slots))
    before = jnp.where((group0 == group1) & (r1 < r0), 1.0, 0.0).astype(bf16)
    start = dot(before, total.astype(bf16))
    dest[...] = jnp.where(hit > 0.0, start + inside - 1.0, -1.0).astype(jnp.int32)
    line = lax.broadcasted_iota(jnp.int32, hit.shape, 0)
    lane = lax.broadcasted_iota(jnp.int32, hit.shape, 1)
    last = jnp.where(line == lane * slots + (slots - 1), start + total, 0.0)
    count[...] = jnp.sum(last, axis=0, keepdims=True).astype(jnp.int32)


def set_places(place, dest, b, c):
    atoms = dest.shape[1]
    slots = place.shape[1] // atoms
    to = dest[pl.ds(pl.multiple_of(b * slots, slots), slots), :]
    row = lax.broadcasted_iota(jnp.int32, (atoms, atoms), 0) + c * atoms
    for q in range(slots):
        hit = jnp.where(to[q : q + 1, :] == row, 1.0, 0.0)
        place[:, q * atoms : (q + 1) * atoms] = hit.astype(bf16)


def plan(count, plan_ref, blocks, atoms):
    def of_block(b, n):
        chunks = (count[0, b] + (atoms - 1)) // atoms

        def of_chunk(c, n):
            plan_ref[0, n] = b
            plan_ref[1, n] = c
            return n + 1

        return lax.fori_loop(0, chunks, of_chunk, n)

    total = lax.fori_loop(0, blocks, of_block, 0)
    plan_ref[0, total] = 0
    plan_ref[1, total] = 0
    return total


def pipelined(total, plan_ref, begin, middle, end):
    begin(0, plan_ref[0, 0], plan_ref[1, 0])

    def step(n, carry):
        before = jnp.maximum(n - 1, 0)
        end(n + 3, plan_ref[0, before])
        middle(n, plan_ref[0, n], plan_ref[1, n])
        begin(n + 1, plan_ref[0, n + 1], plan_ref[1, n + 1])
        return carry

    lax.fori_loop(0, total, step, 0)
    end(total + 3, plan_ref[0, total - 1])


def mix_rows(embedding, w_send, w_radial):
    kinds, channels = embedding.shape
    rows = dot(embedding[...], w_send[0]).astype(bf16).astype(f32)
    row = lax.broadcasted_iota(jnp.int32, (8, channels), 0)
    tile = jnp.zeros((8, channels), f32)
    for kind in range(1, kinds):
        tile = jnp.where(row == 4 + kind, rows[kind : kind + 1, :], tile)
    return jnp.concatenate([tile * w_radial[0, k : k + 1, :] for k in range(w_radial.shape[1])], axis=0)


def columns(rows, atoms):
    turned = rows.T
    return [jnp.broadcast_to(turned[:, k : k + 1], (turned.shape[0], atoms)) for k in range(rows.shape[0])]


def first_kernel(src, home, count, pos, dest, table, rel, embedding, w_send, w_radial, w_update,
                 h1_out, u1_out, s2_out, listed, place, apart, store, sums, stack, plan_ref):
    blocks, slots = src.shape
    atoms = pos.shape[-1]
    basis_count = store.shape[2] // atoms
    total = plan(count, plan_ref, blocks, atoms)
    sums[...] = jnp.zeros_like(sums)
    listed[3] = jnp.zeros(listed.shape[1:], bf16)
    store[1] = jnp.zeros(store.shape[1:], bf16)

    def begin(n, b, c):
        set_places(place, dest, b, c)
        value = dot_nt(place[...], table[b]).astype(bf16)
        listed[n & 3] = value
        apart[n & 1] = dot(value, rel[b])

    def middle(n, b, c):
        fill_kernel(store.at[n & 1], apart.at[n & 1], c, basis_count)

    def end(n, b):
        sums[b] += dot_tn(listed[n & 3][:, :8], store[n & 1])

    pipelined(total, plan_ref, begin, middle, end)
    row = lax.broadcasted_iota(jnp.int32, (embedding.shape[0], atoms), 0).astype(f32)
    species = [pos[home[b]][3:4, :] for b in range(blocks)]
    kinds = side([jnp.where(row == one, 1.0, 0.0) for one in species]).astype(bf16)
    for b in range(blocks):
        for k in range(basis_count):
            stack[k * 8 : (k + 1) * 8, b * atoms : (b + 1) * atoms] = sums[b, :, k * atoms : (k + 1) * atoms]
    mix = mix_rows(embedding, w_send, w_radial)
    message = lax.dot_general(
        mix, stack[...], (((0,), (0,)), ((), ())), preferred_element_type=f32, precision=lax.Precision.HIGHEST
    )
    update = dot_tn(w_update[0], message.astype(bf16))
    hidden = (dot_tn(embedding[...], kinds) + update * jax.nn.sigmoid(update)).astype(bf16)
    sender = jnp.where(side(species) > 0.0, dot_tn(w_send[1], hidden), 0.0).astype(bf16)
    for b in range(blocks):
        there = slice(b * atoms, (b + 1) * atoms)
        h1_out[b] = hidden[:, there]
        u1_out[b] = update[:, there]
        s2_out[b] = sender[:, there]


def set_table(full, table, s2, src):
    blocks, slots = src.shape
    atoms = s2.shape[2]
    full[:, :FEATS, :] = table[...]
    for b in range(blocks):
        for q in range(slots):
            full[b, FEATS:, q * atoms : (q + 1) * atoms] = s2[src[b, q]]


def second_kernel(src, home, count, pos, dest, table, rel, s2, h1, w_radial, w_update, w_out,
                  energy, g2_out, dh2_out, ds_out, full, listed, place, apart, store, acc, sums, wide,
                  both, plan_ref):
    blocks, slots = src.shape
    channels, atoms = s2.shape[1:]
    basis_count = w_radial.shape[1]
    total = plan(count, plan_ref, blocks, atoms)
    set_table(full, table, s2, src)
    sums[...] = jnp.zeros_like(sums)
    listed[3] = jnp.zeros(listed.shape[1:], bf16)
    store[0] = jnp.zeros(store.shape[1:], bf16)

    def begin(n, b, c):
        set_places(place.at[n & 1], dest, b, c)
        value = dot_nt(place[n & 1], full[b]).astype(bf16)
        listed[n & 3] = value
        apart[n & 1] = dot(value[:, :FEATS], rel[b])

    def middle(n, b, c):
        fill_kernel(store.at[n], apart.at[n & 1], c, basis_count)

    def end(n, b):
        sums[b] += dot_tn(listed[n & 3][:, FEATS:], store[jnp.maximum(n - 4, 0)])

    pipelined(total, plan_ref, begin, middle, end)
    radial = columns(w_radial[1], atoms)
    message = side([narrowed(radial, sums.at[b]) for b in range(blocks)])
    up = dot_tn(w_update[1], message.astype(bf16))
    second = side([h1[b] for b in range(blocks)]).astype(f32) + up * jax.nn.sigmoid(up)
    hidden = dot_tn(w_out[...], second.astype(bf16))
    real = side([pos[home[b]][3:4, :] for b in range(blocks)]) > 0.0
    d_hidden = jnp.where(real, columns(energy[...], blocks * atoms)[0] * silu_grad(hidden), 0.0)
    d_second = held(dot_split(w_out[...], d_hidden))
    g2 = dot_split(w_update[1], d_second * silu_grad(up)).astype(bf16)
    for b in range(blocks):
        there = slice(b * atoms, (b + 1) * atoms)
        dh2_out[b] = d_second[:, there]
        g2_out[b] = g2[:, there]
        turned = g2[:, there].astype(f32).T
        for k in range(basis_count):
            wide[b, k * atoms : (k + 1) * atoms, :] = (turned * w_radial[1, k : k + 1, :]).astype(bf16)
    sums[...] = jnp.zeros_like(sums)
    both[1] = jnp.zeros(both.shape[1:], bf16)
    place[1] = jnp.zeros(place.shape[1:], bf16)

    def scatter(n, carry):
        before = jnp.maximum(n - 1, 0)
        sums[plan_ref[0, before]] += dot_tn(both[(n + 1) & 1], place[(n + 1) & 1])
        both[n & 1] = dot(store[n], wide[plan_ref[0, n]]).astype(bf16)
        set_places(place.at[n & 1], dest, plan_ref[0, n], plan_ref[1, n])
        return carry

    lax.fori_loop(0, total, scatter, 0)
    sums[plan_ref[0, total - 1]] += dot_tn(both[(total + 1) & 1], place[(total + 1) & 1])
    acc[...] = jnp.zeros_like(acc)
    for b in range(blocks):
        for q in range(slots):
            acc[src[b, q]] += sums[b, :, q * atoms : (q + 1) * atoms]
    ds_out[...] = acc[...].astype(bf16)


def third_kernel(src, home, count, pos, dest, table, rel, s2, g2, dh2, ds, u1, embedding, w_send, w_radial, w_update,
                 grad_out, full, place, apart, wide, parts, pulls, back, pull, plan_ref):
    blocks, slots = src.shape
    channels, atoms = s2.shape[1:]
    basis_count = w_radial.shape[1]
    _, _, centers, _ = basis_constants(basis_count)
    total = plan(count, plan_ref, blocks, atoms)
    set_table(full, table, s2, src)
    row16 = lax.broadcasted_iota(jnp.int32, (16, atoms), 0)
    folds = side([jnp.where((row16 == d) | (row16 == 8 + d), 1.0, 0.0) for d in range(3)]).astype(bf16)
    real = side([pos[home[b]][3:4, :] for b in range(blocks)]) > 0.0

    def joined(ref):
        return side([ref[b] for b in range(blocks)])

    dh1 = held(joined(dh2) + dot(w_send[1], joined(ds)))
    du1 = dh1 * silu_grad(joined(u1))
    g1 = jnp.where(real, dot_split(w_update[0], du1), 0.0)
    by_kind = dot_wide(mix_rows(embedding, w_send, w_radial), g1)
    radial = columns(w_radial[1], atoms)
    blank = jnp.zeros((FEATS - 16, atoms), f32)
    for b in range(blocks):
        g2_here = g2[b].astype(f32)
        for k in range(basis_count):
            there = slice(k * atoms, (k + 1) * atoms)
            first = by_kind[k * 8 : (k + 1) * 8, b * atoms : (b + 1) * atoms]
            high = held(first)
            wide[b, :FEATS, there] = jnp.concatenate([high, blank, first - high], axis=0).astype(bf16)
            wide[b, FEATS:, there] = (radial[k] * g2_here).astype(bf16)
    back[...] = jnp.zeros_like(back)
    pull[...] = jnp.zeros_like(pull)
    pulls[1] = jnp.zeros(pulls.shape[1:], bf16)
    place[3] = jnp.zeros(place.shape[1:], bf16)

    def begin(n, b, c):
        set_places(place.at[n & 3], dest, b, c)
        value = dot_nt(place[n & 3], full[b]).astype(bf16)
        apart[n & 1] = dot(value[:, :FEATS], rel[b])
        parts[n & 1] = dot(value, wide[b])

    def middle(n, b, c):
        sides = [jnp.zeros((8, atoms), f32)] * 3
        for row0 in range(0, atoms, CHUNK):
            steps, cut, inv, bell, up, down = geometry(apart.at[n & 1], row0, basis_count)
            plain = jnp.zeros_like(cut)
            moment = jnp.zeros_like(cut)
            for k, value in enumerate(radial_powers(bell, up, down, basis_count)):
                term = value * parts[n & 1, row0 : row0 + CHUNK, k * atoms : (k + 1) * atoms]
                plain = plain + term
                moment = moment + centers[k] * term
            scaled = gamma_width * cut
            size = cut * (moment * (scaled * inv) - plain * (scaled + 2.0 / cut_sq))
            for d in range(3):
                force = size * steps[d]
                pulls[n & 1, row0 : row0 + CHUNK, d * atoms : (d + 1) * atoms] = force.astype(bf16)
                sides[d] = sides[d] + jnp.sum(force.reshape(CHUNK // 8, 8, atoms), axis=0)
        pull[b] += jnp.concatenate(sides, axis=0)

    def end(n, b):
        turned = dot_nt(folds, pulls[n & 1])
        high = held(turned)
        turned = jnp.where(row16 < 8, high, turned - high).astype(bf16)
        back[b] += dot(turned, place[n & 3])

    pipelined(total, plan_ref, begin, middle, end)
    grad_out[...] = jnp.zeros_like(grad_out)
    row8 = lax.broadcasted_iota(jnp.int32, (8, atoms), 0)
    for b in range(blocks):
        for q in range(slots):
            there = slice(q * atoms, (q + 1) * atoms)
            grad_out[src[b, q]] += 2.0 * (back[b, :8, there] + back[b, 8:, there])
        for d in range(3):
            at_target = jnp.sum(pull[b, d * 8 : (d + 1) * 8, :], axis=0, keepdims=True)
            grad_out[home[b]] -= jnp.where(row8 == d, 2.0 * at_target, 0.0)


def call(kernel, outs, scratch, smem, args, limit):
    return pl.pallas_call(
        kernel,
        out_shape=outs,
        in_specs=[pl.BlockSpec(memory_space=pltpu.SMEM)] * len(smem)
        + [pl.BlockSpec(memory_space=pltpu.VMEM)] * len(args),
        out_specs=[pl.BlockSpec(memory_space=pltpu.VMEM)] * len(outs),
        scratch_shapes=scratch,
        compiler_params=pltpu.CompilerParams(vmem_limit_bytes=limit << 20),
    )(*smem, *args)


def local(
    positions,
    velocities,
    species,
    neighbour_blocks,
    embedding,
    w_send,
    w_radial,
    w_update,
    w_out,
    w_energy,
    masses,
):
    grid_x, grid_y, grid_z = positions.shape[:3]
    atoms = positions.shape[-1]
    channels = w_send.shape[-1]
    basis_count = w_radial.shape[1]
    kinds = masses.shape[0]
    blocks = grid_x * grid_y * grid_z
    ext_shape = (grid_x + 2, grid_y + 2, grid_z + 2)
    ext_count = ext_shape[0] * ext_shape[1] * ext_shape[2]
    home = jnp.asarray(
        [
            ((x + 1) * ext_shape[1] + y + 1) * ext_shape[2] + z + 1
            for x in range(grid_x)
            for y in range(grid_y)
            for z in range(grid_z)
        ],
        jnp.int32,
    )
    src, live = slot_tables(neighbour_blocks)
    slots = src.shape[1]
    energy = w_energy[None, :]
    species_row = species.astype(f32)[..., None, :]
    filler = jnp.zeros((grid_x, grid_y, grid_z, 4, atoms), f32)
    wide = basis_count * atoms
    spread = slots * atoms

    def shaped(count, dtype):
        return jax.ShapeDtypeStruct((count, channels, atoms), dtype)

    def grid_of(value):
        return value.reshape((grid_x, grid_y, grid_z) + value.shape[1:])

    def flat(value):
        return value.reshape((-1,) + value.shape[3:])

    def gradient(pos):
        dest, count, table, rel = call(
            list_kernel,
            [
                jax.ShapeDtypeStruct((blocks * slots, atoms), jnp.int32),
                jax.ShapeDtypeStruct((1, atoms), jnp.int32),
                jax.ShapeDtypeStruct((blocks, FEATS, spread), bf16),
                jax.ShapeDtypeStruct((blocks, FEATS, 3 * atoms), bf16),
            ],
            [pltpu.VMEM((blocks * slots, atoms), f32)],
            (src, live, home),
            (pos,),
            8,
        )
        smem = (src, home, count)
        lists = (pos, dest, table, rel)
        chunks = blocks * slots
        plan_ref = pltpu.SMEM((2, chunks + 2), jnp.int32)
        h1, u1, s2_own = call(
            first_kernel,
            [shaped(blocks, bf16), shaped(blocks, f32), shaped(blocks, bf16)],
            [
                pltpu.VMEM((4, atoms, FEATS), bf16),
                pltpu.VMEM((atoms, spread), bf16),
                pltpu.VMEM((2, atoms, 3 * atoms), f32),
                pltpu.VMEM((2, atoms, wide), bf16),
                pltpu.VMEM((blocks, 8, wide), f32),
                pltpu.VMEM((basis_count * 8, blocks * atoms), f32),
                plan_ref,
            ],
            smem,
            lists + (embedding, w_send, w_radial, w_update),
            12,
        )
        s2 = flat(padded(grid_of(s2_own), 1))
        g2, dh2, ds = call(
            second_kernel,
            [shaped(blocks, bf16), shaped(blocks, f32), shaped(ext_count, bf16)],
            [
                pltpu.VMEM((blocks, FEATS + channels, spread), bf16),
                pltpu.VMEM((4, atoms, FEATS + channels), bf16),
                pltpu.VMEM((2, atoms, spread), bf16),
                pltpu.VMEM((2, atoms, 3 * atoms), f32),
                pltpu.VMEM((chunks, atoms, wide), bf16),
                pltpu.VMEM((ext_count, channels, atoms), f32),
                pltpu.VMEM((blocks, channels, max(wide, spread)), f32),
                pltpu.VMEM((blocks, wide, channels), bf16),
                pltpu.VMEM((2, atoms, channels), bf16),
                plan_ref,
            ],
            smem,
            lists + (s2, h1, w_radial, w_update, w_out, energy),
            36,
        )
        ds_own = flat(folded(ds.reshape(ext_shape + ds.shape[1:]), (grid_x, grid_y, grid_z), 2))
        (grad,) = call(
            third_kernel,
            [jax.ShapeDtypeStruct((ext_count, 8, atoms), f32)],
            [
                pltpu.VMEM((blocks, FEATS + channels, spread), bf16),
                pltpu.VMEM((4, atoms, spread), bf16),
                pltpu.VMEM((2, atoms, 3 * atoms), f32),
                pltpu.VMEM((blocks, FEATS + channels, wide), bf16),
                pltpu.VMEM((2, atoms, wide), f32),
                pltpu.VMEM((2, atoms, 3 * atoms), bf16),
                pltpu.VMEM((blocks, 16, spread), f32),
                pltpu.VMEM((blocks, 24, atoms), f32),
                plan_ref,
            ],
            smem,
            lists + (s2, g2, dh2, ds_own, u1, embedding, w_send, w_radial, w_update),
            14,
        )
        return grad.reshape(ext_shape + grad.shape[1:])

    mass = jnp.zeros(species.shape, f32)
    for s in range(kinds):
        mass = jnp.where(species == s, masses[s], mass)
    weight = jnp.where(species > 0, mass, 0.0)
    tile = (grid_x, grid_y, grid_z, 8, atoms)
    inverse = jnp.broadcast_to((1.0 / mass)[..., None, :], tile)
    weight = jnp.broadcast_to(weight[..., None, :], tile)
    start = jnp.concatenate([positions, species_row, filler], axis=3)
    half = jnp.pad(velocities, ((0, 0), (0, 0), (0, 0), (0, 5), (0, 0)))
    pos = padded(start, 0)
    half, travelled, pos = kicked(gradient(flat(pos)), start, half, inverse, 3)
    slot_total = (
        positions.size // 3 * lax.axis_size("gx") * lax.axis_size("gy") * lax.axis_size("gz")
    )
    return (travelled, thermostat(gradient(flat(pos)), half, inverse, weight, slot_total, 4))


def solution(mesh):
    placed = (
        P("gx", "gy", "gz", None, None),
        P("gx", "gy", "gz", None, None),
        P("gx", "gy", "gz", None),
        P("gx", "gy", "gz", None),
        P(),
        P(),
        P(),
        P(),
        P(),
        P(),
        P(),
    )
    return jax.shard_map(
        local,
        mesh=mesh,
        in_specs=placed,
        out_specs=(P("gx", "gy", "gz", None, None), P("gx", "gy", "gz", None, None)),
        check_vma=False,
    )
```

```python
import functools
import math

import jax
import jax.numpy as jnp
from jax import lax
from jax.experimental import pallas as pl
from jax.experimental.pallas import tpu as pltpu
from jax.sharding import PartitionSpec as P

soft_sq = 0.25
cut_sq = 25.0
gamma_width = 2.56
time_step = 1.0
target_slot = 0.25
tiny_eps = 1e-06
LOG2E = math.log2(math.e)
CHUNK = 32
DEPTH = 8
bf16 = jnp.bfloat16
f32 = jnp.float32

SIDES = (("gx", 0), ("gy", 1), ("gz", 2))


MESH = pl.DeviceIdType.MESH


DIRECTIONS = [
    (dx, dy, dz) for dx in (-1, 0, 1) for dy in (-1, 0, 1) for dz in (-1, 0, 1) if dx or dy or dz
]


def around(direction):
    present, place = True, {}
    for (axis, _), step in zip(SIDES, direction):
        if step:
            there = lax.axis_index(axis) + step
            present = present & (there >= 0) & (there < lax.axis_size(axis))
            place[axis] = there
    return present, place


def opposite(direction):
    return tuple(-step for step in direction)


def greet(more=()):
    barrier = pltpu.get_barrier_semaphore()
    expected = len(more)
    for place in more:
        pl.semaphore_signal(barrier, inc=1, device_id=place, device_id_type=MESH)
    for direction in DIRECTIONS:
        present, place = around(direction)

        @pl.when(present)
        def _(place=place):
            pl.semaphore_signal(barrier, inc=1, device_id=place, device_id_type=MESH)

        expected = expected + present.astype(jnp.int32)
    return lambda: pl.semaphore_wait(barrier, expected)


def sent(direction, sizes):
    own, ext = [], []
    for step, size in zip(direction, sizes):
        own.append(pl.ds(0, size) if step == 0 else pl.ds(0 if step < 0 else size - 1, 1))
        ext.append(pl.ds(1, size) if step == 0 else pl.ds(size + 1 if step < 0 else 0, 1))
    return tuple(own), tuple(ext)


def rim(direction, sizes):
    return tuple(
        pl.ds(1, size) if step == 0 else pl.ds(0 if step < 0 else size + 1, 1)
        for step, size in zip(direction, sizes)
    )


def exchange(pairs, send_sem, recv_sem):
    copies = []
    for at, (direction, (source, target)) in enumerate(zip(DIRECTIONS, pairs)):
        present, place = around(direction)
        copy = pltpu.make_async_remote_copy(
            src_ref=source,
            dst_ref=target,
            send_sem=send_sem.at[at],
            recv_sem=recv_sem.at[at],
            device_id=place,
            device_id_type=MESH,
        )
        pl.when(present)(copy.start)
        copies.append((copy, present, around(opposite(direction))[0]))

    def finish():
        for copy, _, arrives in copies:
            pl.when(arrives)(copy.wait_recv)
        for copy, present, _ in copies:
            pl.when(present)(copy.wait_send)

    return finish


def blank_rim(ext, sizes):
    for direction in DIRECTIONS:

        @pl.when(jnp.logical_not(around(direction)[0]))
        def _(direction=direction):
            index = rim(direction, sizes)
            ext[index] = jnp.zeros(tuple(part.size for part in index) + ext.shape[3:], ext.dtype)


def spread_rim(own, ext, sizes, send_sem, recv_sem):
    pairs = []
    for direction in DIRECTIONS:
        mine, theirs = sent(direction, sizes)
        pairs.append((own.at[mine], ext.at[theirs]))
    return exchange(pairs, send_sem, recv_sem)


def halo_kernel(own, ext, send_sem, recv_sem, copy_sem):
    ready = greet()
    sizes = own.shape[:3]
    fill = pltpu.make_async_copy(own, ext.at[tuple(pl.ds(1, size) for size in sizes)], copy_sem)
    fill.start()
    blank_rim(ext, sizes)
    ready()
    finish = spread_rim(own, ext, sizes, send_sem, recv_sem)
    fill.wait()
    finish()


def start_kernel(positions, species, ext, send_sem, recv_sem, copy_sem, fresh):
    sizes = fresh.shape[:3]
    for x, y, z in cells_of(sizes):
        rows = [positions[x, y, d, z : z + 1, :] for d in range(3)]
        fresh[x, y, z] = tile_of(rows + [species[x, y, z : z + 1, :].astype(f32)])
    halo_kernel(fresh, ext, send_sem, recv_sem, copy_sem)


def tile_of(rows):
    row = lax.broadcasted_iota(jnp.int32, (8, rows[0].shape[-1]), 0)
    tile = jnp.zeros(row.shape, f32)
    for at, value in enumerate(rows):
        tile = jnp.where(row == at, value, tile)
    return tile


def mass_of(species, masses):
    mass = jnp.full(species.shape, masses[0], f32)
    for kind in range(1, masses.shape[0]):
        mass = jnp.where(species == kind, masses[kind], mass)
    return mass


def landing_scratch(sizes, tail, dtype):
    return [
        pltpu.VMEM(tuple(1 if step else size for step, size in zip(direction, sizes)) + tail, dtype)
        for direction in DIRECTIONS
    ]


def blank_lands(lands):
    for direction, land in zip(DIRECTIONS, lands):

        @pl.when(jnp.logical_not(around(opposite(direction))[0]))
        def _(land=land):
            land[...] = jnp.zeros_like(land)


def gather_rim(ext, lands, sizes, send_sem, recv_sem):
    pairs = [(ext.at[rim(direction, sizes)], land) for direction, land in zip(DIRECTIONS, lands)]
    return exchange(pairs, send_sem, recv_sem)


def cells_of(sizes):
    return [(x, y, z) for x in range(sizes[0]) for y in range(sizes[1]) for z in range(sizes[2])]


def landed(ext, lands, sizes, cell):
    value = ext[tuple(at + 1 for at in cell)].astype(f32)
    for direction, land in zip(DIRECTIONS, lands):
        index = []
        for step, size, at in zip(direction, sizes, cell):
            if step == 0:
                index.append(at)
            elif at == (size - 1 if step < 0 else 0):
                index.append(0)
        if len(index) == 3:
            value = value + land[tuple(index)].astype(f32)
    return value


def fold_kernel(ext, own, *refs):
    lands, (send_sem, recv_sem) = refs[:26], refs[26:]
    ready = greet()
    sizes = own.shape[:3]
    blank_lands(lands)
    ready()
    gather_rim(ext, lands, sizes, send_sem, recv_sem)()
    for cell in cells_of(sizes):
        own[cell] = landed(ext, lands, sizes, cell).astype(own.dtype)


def kick_kernel(masses, ext, positions, velocities, species, out_half, out_moved, out_pos, *refs):
    lands, (send_sem, recv_sem, send_two, recv_two, copy_sem, fresh) = refs[:26], refs[26:]
    ready = greet()
    sizes = fresh.shape[:3]
    blank_lands(lands)
    blank_rim(out_pos, sizes)
    ready()
    gather_rim(ext, lands, sizes, send_sem, recv_sem)()
    for cell in cells_of(sizes):
        x, y, z = cell
        kinds = species[x, y, z : z + 1, :]
        force = -landed(ext, lands, sizes, cell) * (0.5 * time_step / mass_of(kinds, masses))
        rows = []
        for d in range(3):
            half_kick = velocities[x, y, d, z : z + 1, :] + force[d : d + 1, :]
            moved = time_step * half_kick
            out_half[x, y, d, z : z + 1, :] = half_kick
            out_moved[x, y, d, z : z + 1, :] = moved
            rows.append(positions[x, y, d, z : z + 1, :] + moved)
        fresh[cell] = tile_of(rows + [kinds.astype(f32)])
    fill = pltpu.make_async_copy(fresh, out_pos.at[tuple(pl.ds(1, size) for size in sizes)], copy_sem)
    fill.start()
    finish = spread_rim(fresh, out_pos, sizes, send_two, recv_two)
    fill.wait()
    finish()


def ring(axes):
    steps = [()]
    for axis in axes:
        steps = [step + (t,) for step in steps for t in range(lax.axis_size(axis))]
    places = []
    for step in steps[1:]:
        places.append(
            {axis: lax.rem(lax.axis_index(axis) + t, lax.axis_size(axis)) for axis, t in zip(axes, step) if t}
        )
    return places


STAGES = (("gx", "gy"), ("gz",))


def last_kernel(slot_total, masses, ext, half, species, out, *refs):
    lands, refs = refs[:26], refs[26:]
    send_sem, recv_sem, send_two, recv_two, speed = refs[:5]
    inbox, sums = refs[5:7], refs[7:9]
    ready = greet([place for axes in STAGES for place in ring(axes)])
    sizes = speed.shape[:3]
    blank_lands(lands)
    ready()
    gather_rim(ext, lands, sizes, send_sem, recv_sem)()
    total = jnp.zeros(speed.shape[3:], f32)
    for cell in cells_of(sizes):
        x, y, z = cell
        kinds = species[x, y, z : z + 1, :]
        mass = mass_of(kinds, masses)
        force = -landed(ext, lands, sizes, cell) * (0.5 * time_step / mass)
        velocity = tile_of([half[x, y, d, z : z + 1, :] + force[d : d + 1, :] for d in range(3)])
        speed[cell] = velocity
        total = total + jnp.where(kinds > 0, 0.5 * mass, 0.0) * velocity * velocity
    base = 0
    for stage, axes in enumerate(STAGES):
        sums[stage][...] = total
        copies = []
        for t, place in enumerate(ring(axes)):
            copy = pltpu.make_async_remote_copy(
                src_ref=sums[stage],
                dst_ref=inbox[stage].at[t],
                send_sem=send_two.at[base],
                recv_sem=recv_two.at[base],
                device_id=place,
                device_id_type=MESH,
            )
            copy.start()
            copies.append(copy)
            base += 1
        for t, copy in enumerate(copies):
            copy.wait()
            total = total + inbox[stage][t]
    kinetic = jnp.sum(total, keepdims=True)
    factor = jnp.sqrt(target_slot * slot_total / (kinetic + tiny_eps))
    for x, y, z in cells_of(sizes):
        value = speed[x, y, z] * factor
        for d in range(3):
            out[x, y, d, z : z + 1, :] = value[d : d + 1, :]


def vmem_specs(count):
    return [pl.BlockSpec(memory_space=pltpu.VMEM)] * count


def remote_call(kernel, outs, scratch, collective_id, args, smem=()):
    return pl.pallas_call(
        kernel,
        out_shape=outs,
        in_specs=[pl.BlockSpec(memory_space=pltpu.SMEM)] * len(smem) + vmem_specs(len(args)),
        out_specs=vmem_specs(len(outs)),
        scratch_shapes=scratch,
        compiler_params=pltpu.CompilerParams(
            collective_id=collective_id, has_side_effects=True, vmem_limit_bytes=12 << 20
        ),
    )(*smem, *args)


def semaphores():
    return [pltpu.SemaphoreType.DMA((26,)), pltpu.SemaphoreType.DMA((26,))]


def padded_shape(shape, dtype):
    return jax.ShapeDtypeStruct(tuple(size + 2 for size in shape[:3]) + shape[3:], dtype)


def padded(cells, collective_id):
    scratch = semaphores() + [pltpu.SemaphoreType.DMA]
    return remote_call(halo_kernel, [padded_shape(cells.shape, cells.dtype)], scratch, collective_id, (cells,))[0]


def tiles_shape(species):
    return species.shape[:3] + (8,) + species.shape[3:]


def started(positions, species, collective_id):
    tiles = tiles_shape(species)
    scratch = semaphores() + [pltpu.SemaphoreType.DMA, pltpu.VMEM(tiles, f32)]
    return remote_call(start_kernel, [padded_shape(tiles, f32)], scratch, collective_id, (positions, species))[0]


def folded(grid, sizes, collective_id):
    tail = grid.shape[3:]
    scratch = landing_scratch(sizes, tail, grid.dtype) + semaphores()
    out = jax.ShapeDtypeStruct(sizes + tail, grid.dtype)
    return remote_call(fold_kernel, [out], scratch, collective_id, (grid,))[0]


def kicked(grid, positions, velocities, species, masses, collective_id):
    tiles = tiles_shape(species)
    scratch = landing_scratch(tiles[:3], tiles[3:], f32) + semaphores() + semaphores()
    scratch += [pltpu.SemaphoreType.DMA, pltpu.VMEM(tiles, f32)]
    raw = jax.ShapeDtypeStruct(positions.shape, f32)
    outs = [raw, raw, padded_shape(tiles, f32)]
    return remote_call(kick_kernel, outs, scratch, collective_id, (grid, positions, velocities, species), (masses,))


def thermostat(grid, half, species, masses, slot_total, collective_id):
    tiles = tiles_shape(species)
    counts = [math.prod(lax.axis_size(axis) for axis in axes) for axes in STAGES]
    peers = sum(count - 1 for count in counts)
    scratch = landing_scratch(tiles[:3], tiles[3:], f32) + semaphores()
    scratch += [pltpu.SemaphoreType.DMA((peers,)), pltpu.SemaphoreType.DMA((peers,)), pltpu.VMEM(tiles, f32)]
    scratch += [pltpu.VMEM((max(count - 1, 1),) + tiles[3:], f32) for count in counts]
    scratch += [pltpu.VMEM(tiles[3:], f32)] * 2
    out = jax.ShapeDtypeStruct(half.shape, f32)
    kernel = functools.partial(last_kernel, float(slot_total))
    return remote_call(kernel, [out], scratch, collective_id, (grid, half, species), (masses,))[0]


def slot_tables(neighbour_blocks):
    size_x, size_y, size_z, slot_count = neighbour_blocks.shape
    is_live = neighbour_blocks < 27
    offset = jnp.where(is_live, neighbour_blocks, 13)
    index_x = lax.broadcasted_iota(jnp.int32, neighbour_blocks.shape, 0)
    index_y = lax.broadcasted_iota(jnp.int32, neighbour_blocks.shape, 1)
    index_z = lax.broadcasted_iota(jnp.int32, neighbour_blocks.shape, 2)
    source = (
        (index_x + offset // 9) * (size_y + 2) + (index_y + offset // 3 % 3)
    ) * (size_z + 2) + (index_z + offset % 3)
    return source.reshape(-1, slot_count)


def basis_constants(basis_count):
    step = 5.0 / basis_count
    mid = basis_count // 2
    centers = [(k + 0.5) * step for k in range(basis_count)]
    scales = [math.exp(-gamma_width * (centers[k] - centers[mid]) ** 2) for k in range(basis_count)]
    return step, mid, centers, scales


def geometry(apart, row0, basis_count):
    step, mid, centers, _ = basis_constants(basis_count)
    atoms = apart.shape[1] // 3
    rows = slice(row0, row0 + CHUNK)
    steps = [apart[rows, d * atoms : (d + 1) * atoms] for d in range(3)]
    dx, dy, dz = steps
    squared = jnp.minimum(dx * dx + dy * dy + dz * dz, cut_sq)
    cut = 1.0 - squared * (1.0 / cut_sq)
    soft = squared + soft_sq
    inv = lax.rsqrt(soft)
    shift = soft * inv - centers[mid]
    bell = jnp.exp2((-gamma_width * LOG2E) * (shift * shift))
    slope = shift * (2.0 * gamma_width * step * LOG2E)
    return steps, cut, inv, bell, jnp.exp2(slope), jnp.exp2(-slope)


def radial_powers(start, up, down, basis_count):
    mid = basis_count // 2
    powers = [None] * basis_count
    powers[mid] = start
    for k in range(mid + 1, basis_count):
        powers[k] = powers[k - 1] * up
    for k in range(mid - 1, -1, -1):
        powers[k] = powers[k + 1] * down
    scales = basis_constants(basis_count)[3]
    return [power * scale if scale != 1.0 else power for power, scale in zip(powers, scales)]


def fill_kernel(store, apart, c, basis_count):
    rows, atoms = apart.shape[0], apart.shape[1] // 3
    for row0 in range(0, rows, CHUNK):
        _, cut, _, bell, up, down = geometry(apart, row0, basis_count)
        ahead = lax.broadcasted_iota(jnp.int32, cut.shape, 1) - lax.broadcasted_iota(jnp.int32, cut.shape, 0)
        cut = jnp.where(ahead == row0 + c * rows, 0.0, cut)
        for k, value in enumerate(radial_powers(cut * cut * bell, up, down, basis_count)):
            store[row0 : row0 + CHUNK, k * atoms : (k + 1) * atoms] = value.astype(bf16)


def split(value):
    high = value.astype(bf16)
    return high, (value - high.astype(f32)).astype(bf16)


def dot_split(a, value):
    high, low = split(value)
    return dot(a, high) + dot(a, low)


def held(value):
    return value.astype(bf16).astype(f32)


def narrowed(radial, sums):
    atoms = radial[0].shape[-1]
    return sum(column * sums[:, k * atoms : (k + 1) * atoms] for k, column in enumerate(radial))


def silu_grad(value):
    gate = jax.nn.sigmoid(value)
    return gate * (1.0 + value * (1.0 - gate))


def dot(a, b):
    return jnp.dot(a, b, preferred_element_type=f32)


def dot_wide(a, b):
    return jnp.dot(a, b, preferred_element_type=f32, precision=lax.Precision.HIGHEST)


def dot_nt(a, b):
    return lax.dot_general(a, b, (((1,), (1,)), ((), ())), preferred_element_type=f32)


def dot_tn(a, b):
    return lax.dot_general(a, b, (((0,), (0,)), ((), ())), preferred_element_type=f32)


FEATS = 32


def thirds(value):
    high = held(value)
    rest = value - high
    mid = held(rest)
    return high, mid, rest - mid


def side(values):
    return jnp.concatenate(values, axis=1)


def features(block, origin):
    row = lax.broadcasted_iota(jnp.int32, block.shape, 0)
    where = jnp.where(row < 3, block - origin, 0.0)
    square = jnp.sum(where * where, axis=0, keepdims=True) * near_part
    high = held(square)
    tiles = [jnp.where(row < 3, part, jnp.where(row == 3, 1.0, 0.0)) for part in thirds(where)]
    again = pltpu.roll(jnp.where(row < 3, tiles[0], 0.0), 4, 0)
    kinds = jnp.where((row > 3) & (block[3:4, :] == row.astype(f32) - 4.0), 1.0, 0.0)
    tiles[0] = jnp.where(row > 3, kinds, tiles[0])
    tiles[1] = jnp.where(row == 4, high, jnp.where(row == 5, square - high, tiles[1]))
    tiles[2] = tiles[2] + again
    return jnp.concatenate(tiles + [kinds], axis=0).astype(bf16)


near_part = 1.0 - 2.0**-13


def reach_rows(own, origin):
    row = lax.broadcasted_iota(jnp.int32, own.shape, 0)
    where = jnp.where(row < 3, own - origin, 0.0)
    square = jnp.sum(where * where, axis=0, keepdims=True) * near_part
    square = jnp.where(own[3:4, :] > 0.0, square, 1e9)
    top = held(square)
    high, mid, _ = thirds(where)
    tiles = [
        jnp.where(row == 3, top, -2.0 * high),
        jnp.where(row == 3, square - top, jnp.where((row == 4) | (row == 5), 1.0, -2.0 * high)),
        pltpu.roll(-2.0 * mid, 4, 0),
        jnp.zeros_like(own),
    ]
    return jnp.concatenate(tiles, axis=0).astype(bf16)


def set_apart(rel, own, origin):
    atoms = own.shape[-1]
    row = lax.broadcasted_iota(jnp.int32, (FEATS, atoms), 0)
    high, mid, low = thirds(own - origin)
    for d in range(3):
        tile = jnp.where((row == d) | (row == 8 + d) | (row == 16 + d), 1.0, 0.0)
        for at, part in ((3, high), (11, mid), (19, low)):
            tile = jnp.where(row == at, -part[d : d + 1, :], tile)
        rel[:, d * atoms : (d + 1) * atoms] = tile.astype(bf16)


def list_kernel(home, src, pos, dest, count, table, rel, hits):
    blocks, slots = src.shape
    atoms = pos.shape[-1]
    origin = pos[home[0]][:, 0:1]
    for b in range(blocks):
        own = pos[home[b]]
        set_apart(rel.at[b], own, origin)
        for q in range(slots):
            table[b, :, q * atoms : (q + 1) * atoms] = features(pos[src[b, q]], origin)
    for b in range(blocks):
        reach = dot_tn(reach_rows(pos[home[b]], origin), table[b])
        reach = jnp.min(reach, axis=0, keepdims=True)
        for q in range(slots):
            live = 1.0 if q == 0 else (src[b, q] != home[b]).astype(f32)
            real = pos[src[b, q]][3:4, :] > 0.0
            near = (reach[:, q * atoms : (q + 1) * atoms] < cut_sq * 1.001) & real
            hits[b * slots + q : b * slots + q + 1, :] = jnp.where(near, live, 0.0)
    hit = hits[...]
    shape = (atoms, atoms)
    upto = lax.broadcasted_iota(jnp.int32, shape, 0) <= lax.broadcasted_iota(jnp.int32, shape, 1)
    inside = dot(hit.astype(bf16), jnp.where(upto, 1.0, 0.0).astype(bf16))
    total = jnp.broadcast_to(inside[:, atoms - 1 : atoms], hit.shape)
    pairs = blocks * slots
    r0 = lax.broadcasted_iota(jnp.int32, (pairs, pairs), 0)
    r1 = lax.broadcasted_iota(jnp.int32, (pairs, pairs), 1)
    group0 = jnp.floor((r0.astype(f32) + 0.5) * (1.0 / slots))
    group1 = jnp.floor((r1.astype(f32) + 0.5) * (1.0 / slots))
    before = jnp.where((group0 == group1) & (r1 < r0), 1.0, 0.0).astype(bf16)
    start = dot(before, total.astype(bf16))
    dest[...] = jnp.where(hit > 0.0, start + inside - 1.0, -1.0).astype(jnp.int32)
    line = lax.broadcasted_iota(jnp.int32, hit.shape, 0)
    lane = lax.broadcasted_iota(jnp.int32, hit.shape, 1)
    last = jnp.where(line == lane * slots + (slots - 1), start + total, 0.0)
    count[...] = jnp.sum(last, axis=0, keepdims=True).astype(jnp.int32)


def set_places(place, dest, b, c):
    rows, atoms = place.shape[0], dest.shape[1]
    slots = place.shape[1] // atoms
    to = dest[pl.ds(pl.multiple_of(b * slots, slots), slots), :]
    to = jnp.clip(to - c * rows, -1, rows).astype(f32)
    row = lax.broadcasted_iota(jnp.int32, (rows, atoms), 0).astype(f32).astype(bf16)
    one, none = jnp.ones((rows, atoms), bf16), jnp.zeros((rows, atoms), bf16)
    for q in range(slots):
        here = jnp.broadcast_to(to[q : q + 1, :], (rows, atoms)).astype(bf16)
        place[:, q * atoms : (q + 1) * atoms] = jnp.where(here == row, one, none)


def plan(count, plan_ref, blocks, rows):
    def of_block(b, n):
        chunks = (count[0, b] + (rows - 1)) // rows

        def of_chunk(c, n):
            plan_ref[0, n] = b
            plan_ref[1, n] = c
            return n + 1

        return lax.fori_loop(0, chunks, of_chunk, n)

    end = lax.fori_loop(0, blocks, of_block, DEPTH)
    for t in range(DEPTH):
        for at in (t, end + t):
            plan_ref[0, at] = 0
            plan_ref[1, at] = 0
    return end - DEPTH


def pipelined(total, plan_ref, stages):
    def step(t, carry):
        for s in range(len(stages) - 1, -1, -1):
            n = t - s
            stages[s](n, plan_ref[0, n + DEPTH], plan_ref[1, n + DEPTH], (n >= 0) & (n < total))
        return carry

    lax.fori_loop(0, total + len(stages) - 1, step, 0)


def mix_rows(embedding, w_send, w_radial):
    kinds, channels = embedding.shape
    rows = dot(embedding[...], w_send[0]).astype(bf16).astype(f32)
    row = lax.broadcasted_iota(jnp.int32, (8, channels), 0)
    tile = jnp.zeros((8, channels), f32)
    for kind in range(1, kinds):
        tile = jnp.where(row == 4 + kind, rows[kind : kind + 1, :], tile)
    return jnp.concatenate([tile * w_radial[0, k : k + 1, :] for k in range(w_radial.shape[1])], axis=0)


def columns(rows, atoms):
    turned = rows.T
    return [jnp.broadcast_to(turned[:, k : k + 1], (turned.shape[0], atoms)) for k in range(rows.shape[0])]


def first_kernel(home, src, count, pos, dest, table, rel, embedding, w_send, w_radial, w_update,
                 h1_out, u1_out, s2_out, listed, place, apart, store, sums, stack, plan_ref):
    blocks, slots = src.shape
    atoms = pos.shape[-1]
    basis_count = store.shape[2] // atoms
    total = plan(count, plan_ref, blocks, store.shape[1])
    sums[...] = jnp.zeros_like(sums)

    def places(n, b, c, valid):
        set_places(place.at[n & 1], dest, b, c)

    def gather(n, b, c, valid):
        listed[n & 3] = dot_nt(place[n & 1], table[b]).astype(bf16)

    def differ(n, b, c, valid):
        apart[n & 1] = dot(listed[n & 3], rel[b])

    def fill(n, b, c, valid):
        fill_kernel(store.at[n & 1], apart.at[n & 1], c, basis_count)

    def collect(n, b, c, valid):
        sums[b] += jnp.where(valid, dot_tn(listed[n & 3][:, :8], store[n & 1]), 0.0)

    pipelined(total, plan_ref, [places, gather, differ, fill, collect])
    row = lax.broadcasted_iota(jnp.int32, (embedding.shape[0], atoms), 0).astype(f32)
    species = [pos[home[b]][3:4, :] for b in range(blocks)]
    kinds = side([jnp.where(row == one, 1.0, 0.0) for one in species]).astype(bf16)
    for b in range(blocks):
        for k in range(basis_count):
            stack[k * 8 : (k + 1) * 8, b * atoms : (b + 1) * atoms] = sums[b, :, k * atoms : (k + 1) * atoms]
    mix = mix_rows(embedding, w_send, w_radial)
    message = lax.dot_general(
        mix, stack[...], (((0,), (0,)), ((), ())), preferred_element_type=f32, precision=lax.Precision.HIGHEST
    )
    update = dot_tn(w_update[0], message.astype(bf16))
    hidden = (dot_tn(embedding[...], kinds) + update * jax.nn.sigmoid(update)).astype(bf16)
    sender = jnp.where(side(species) > 0.0, dot_tn(w_send[1], hidden), 0.0).astype(bf16)
    for b in range(blocks):
        there = slice(b * atoms, (b + 1) * atoms)
        h1_out[b] = hidden[:, there]
        u1_out[b] = update[:, there]
        s2_out[b] = sender[:, there]


def set_table(full, table, s2, src):
    blocks, slots = src.shape
    atoms = s2.shape[2]
    channels = s2.shape[1]
    full[:, channels:, :] = table[...]
    for b in range(blocks):
        for q in range(slots):
            full[b, :channels, q * atoms : (q + 1) * atoms] = s2[src[b, q]]


def second_kernel(home, src, count, pos, dest, table, rel, s2, h1, w_radial, w_update, w_out,
                  energy, g2_out, dh2_out, ds_out, listed, wide_rel, full, place, apart, store, acc, sums, wide,
                  both, plan_ref):
    blocks, slots = src.shape
    channels, atoms = s2.shape[1:]
    basis_count = w_radial.shape[1]
    total = plan(count, plan_ref, blocks, store.shape[1])
    set_table(full, table, s2, src)
    wide_rel[:, :channels, :] = jnp.zeros((blocks, channels, rel.shape[2]), bf16)
    wide_rel[:, channels:, :] = rel[...]
    sums[...] = jnp.zeros_like(sums)
    spare = store.shape[0] - 1

    def held_at(n, valid):
        return jnp.where(valid, n, spare)

    def places(n, b, c, valid):
        set_places(place.at[n & 1], dest, b, c)

    def gather(n, b, c, valid):
        listed[held_at(n, valid)] = dot_nt(place[n & 1], full[b]).astype(bf16)

    def differ(n, b, c, valid):
        apart[n & 1] = dot(listed[held_at(n, valid)], wide_rel[b])

    def fill(n, b, c, valid):
        fill_kernel(store.at[held_at(n, valid)], apart.at[n & 1], c, basis_count)

    def collect(n, b, c, valid):
        at = held_at(n, valid)
        sums[b] += jnp.where(valid, dot_tn(listed[at][:, :channels], store[at]), 0.0)

    pipelined(total, plan_ref, [places, gather, differ, fill, collect])
    radial = columns(w_radial[1], atoms)
    message = side([narrowed(radial, sums.at[b]) for b in range(blocks)])
    up = dot_tn(w_update[1], message.astype(bf16))
    second = side([h1[b] for b in range(blocks)]).astype(f32) + up * jax.nn.sigmoid(up)
    hidden = dot_tn(w_out[...], second.astype(bf16))
    real = side([pos[home[b]][3:4, :] for b in range(blocks)]) > 0.0
    d_hidden = jnp.where(real, columns(energy[...], blocks * atoms)[0] * silu_grad(hidden), 0.0)
    d_second = held(dot_split(w_out[...], d_hidden))
    g2 = dot_split(w_update[1], d_second * silu_grad(up)).astype(bf16)
    for b in range(blocks):
        there = slice(b * atoms, (b + 1) * atoms)
        dh2_out[b] = d_second[:, there]
        g2_out[b] = g2[:, there]
        turned = g2[:, there].astype(f32).T
        for k in range(basis_count):
            wide[b, k * atoms : (k + 1) * atoms, :] = (turned * w_radial[1, k : k + 1, :]).astype(bf16)
    sums[...] = jnp.zeros_like(sums)

    def project(n, b, c, valid):
        both[n & 1] = dot(store[held_at(n, valid)], wide[b]).astype(bf16)
        set_places(place.at[n & 1], dest, b, c)

    def scatter(n, b, c, valid):
        sums[b] += jnp.where(valid, dot_tn(both[n & 1], place[n & 1]), 0.0)

    pipelined(total, plan_ref, [project, scatter])
    acc[...] = jnp.zeros_like(acc)
    for b in range(blocks):
        for q in range(slots):
            acc[src[b, q]] += sums[b, :, q * atoms : (q + 1) * atoms]
    ds_out[...] = acc[...].astype(bf16)


def third_kernel(home, src, count, pos, dest, rel, listed, g2, dh2, ds, u1, embedding, w_send, w_radial, w_update,
                 grad_out, place, apart, wide, parts, pulls, turned, back, pull, plan_ref):
    blocks, slots = src.shape
    channels, atoms = g2.shape[1:]
    rows = parts.shape[1]
    basis_count = w_radial.shape[1]
    _, _, centers, _ = basis_constants(basis_count)
    total = plan(count, plan_ref, blocks, rows)
    row16 = lax.broadcasted_iota(jnp.int32, (16, rows), 0)
    unit = lax.broadcasted_iota(jnp.int32, (16, atoms), 0)
    folds = side([jnp.where((unit == d) | (unit == 8 + d), 1.0, 0.0) for d in range(3)]).astype(bf16)
    real = side([pos[home[b]][3:4, :] for b in range(blocks)]) > 0.0

    def joined(ref):
        return side([ref[b] for b in range(blocks)])

    dh1 = held(joined(dh2) + dot(w_send[1], joined(ds)))
    du1 = dh1 * silu_grad(joined(u1))
    g1 = jnp.where(real, dot_split(w_update[0], du1), 0.0)
    by_kind = dot_wide(mix_rows(embedding, w_send, w_radial), g1)
    radial = columns(w_radial[1], atoms)
    blank = jnp.zeros((FEATS - 16, atoms), f32)
    for b in range(blocks):
        g2_here = g2[b].astype(f32)
        for k in range(basis_count):
            there = slice(k * atoms, (k + 1) * atoms)
            first = by_kind[k * 8 : (k + 1) * 8, b * atoms : (b + 1) * atoms]
            high = held(first)
            wide[b, channels:, there] = jnp.concatenate([high, blank, first - high], axis=0).astype(bf16)
            wide[b, :channels, there] = (radial[k] * g2_here).astype(bf16)
    back[...] = jnp.zeros_like(back)
    pull[...] = jnp.zeros_like(pull)

    def differ(n, b, c, valid):
        at = jnp.where(valid, n, 0)
        apart[n & 1] = dot(listed[at], rel[b])
        parts[n & 1] = dot(listed[at], wide[b])

    def pair(n, b, c, valid):
        sides = [jnp.zeros((8, atoms), f32)] * 3
        for row0 in range(0, rows, CHUNK):
            steps, cut, inv, bell, up, down = geometry(apart.at[n & 1], row0, basis_count)
            plain = jnp.zeros_like(cut)
            moment = jnp.zeros_like(cut)
            for k, value in enumerate(radial_powers(bell, up, down, basis_count)):
                term = value * parts[n & 1, row0 : row0 + CHUNK, k * atoms : (k + 1) * atoms]
                plain = plain + term
                moment = moment + centers[k] * term
            scaled = gamma_width * cut
            size = cut * (moment * (scaled * inv) - plain * (scaled + 2.0 / cut_sq))
            for d in range(3):
                force = size * steps[d]
                pulls[n & 1, row0 : row0 + CHUNK, d * atoms : (d + 1) * atoms] = force.astype(bf16)
                sides[d] = sides[d] + jnp.sum(force.reshape(CHUNK // 8, 8, atoms), axis=0)
        pull[b] += jnp.where(valid, jnp.concatenate(sides, axis=0), 0.0)

    def turn(n, b, c, valid):
        value = dot_nt(folds, pulls[n & 1])
        high = held(value)
        turned[n & 1] = jnp.where(row16 < 8, high, value - high).astype(bf16)
        set_places(place.at[n & 1], dest, b, c)

    def scatter(n, b, c, valid):
        back[b] += jnp.where(valid, dot(turned[n & 1], place[n & 1]), 0.0)

    pipelined(total, plan_ref, [differ, pair, turn, scatter])
    grad_out[...] = jnp.zeros_like(grad_out)
    row8 = lax.broadcasted_iota(jnp.int32, (8, atoms), 0)
    for b in range(blocks):
        for q in range(slots):
            there = slice(q * atoms, (q + 1) * atoms)
            grad_out[src[b, q]] += 2.0 * (back[b, :8, there] + back[b, 8:, there])
        for d in range(3):
            at_target = jnp.sum(pull[b, d * 8 : (d + 1) * 8, :], axis=0, keepdims=True)
            grad_out[home[b]] -= jnp.where(row8 == d, 2.0 * at_target, 0.0)


def call(kernel, outs, scratch, smem, args, limit):
    return pl.pallas_call(
        kernel,
        out_shape=outs,
        in_specs=[pl.BlockSpec(memory_space=pltpu.SMEM)] * len(smem)
        + [pl.BlockSpec(memory_space=pltpu.VMEM)] * len(args),
        out_specs=[pl.BlockSpec(memory_space=pltpu.VMEM)] * len(outs),
        scratch_shapes=scratch,
        compiler_params=pltpu.CompilerParams(vmem_limit_bytes=limit << 20),
    )(*smem, *args)


def local(
    positions,
    velocities,
    species,
    neighbour_blocks,
    embedding,
    w_send,
    w_radial,
    w_update,
    w_out,
    w_energy,
    masses,
):
    grid_x, grid_y, grid_z = positions.shape[:3]
    atoms = positions.shape[-1]
    channels = w_send.shape[-1]
    basis_count = w_radial.shape[1]
    kinds = masses.shape[0]
    blocks = grid_x * grid_y * grid_z
    ext_shape = (grid_x + 2, grid_y + 2, grid_z + 2)
    ext_count = ext_shape[0] * ext_shape[1] * ext_shape[2]
    home = [
        ((x + 1) * ext_shape[1] + y + 1) * ext_shape[2] + z + 1
        for x in range(grid_x)
        for y in range(grid_y)
        for z in range(grid_z)
    ]
    src = slot_tables(neighbour_blocks)
    slots = src.shape[1]
    energy = w_energy[None, :]
    wide = basis_count * atoms
    spread = slots * atoms

    def shaped(count, dtype):
        return jax.ShapeDtypeStruct((count, channels, atoms), dtype)

    def grid_of(value):
        return value.reshape((grid_x, grid_y, grid_z) + value.shape[1:])

    def flat(value):
        return value.reshape((-1,) + value.shape[3:])

    def gradient(pos):
        dest, count, table, rel = call(
            functools.partial(list_kernel, home),
            [
                jax.ShapeDtypeStruct((blocks * slots, atoms), jnp.int32),
                jax.ShapeDtypeStruct((1, atoms), jnp.int32),
                jax.ShapeDtypeStruct((blocks, FEATS, spread), bf16),
                jax.ShapeDtypeStruct((blocks, FEATS, 3 * atoms), bf16),
            ],
            [pltpu.VMEM((blocks * slots, atoms), f32)],
            (src,),
            (pos,),
            8,
        )
        smem = (src, count)
        lists = (pos, dest, table, rel)
        rows = atoms + atoms // 2
        chunks = blocks * (-(-slots * atoms // rows))
        plan_ref = pltpu.SMEM((2, chunks + 2 * DEPTH), jnp.int32)
        h1, u1, s2_own = call(
            functools.partial(first_kernel, home),
            [shaped(blocks, bf16), shaped(blocks, f32), shaped(blocks, bf16)],
            [
                pltpu.VMEM((4, rows, FEATS), bf16),
                pltpu.VMEM((2, rows, spread), bf16),
                pltpu.VMEM((2, rows, 3 * atoms), f32),
                pltpu.VMEM((2, rows, wide), bf16),
                pltpu.VMEM((blocks, 8, wide), f32),
                pltpu.VMEM((basis_count * 8, blocks * atoms), f32),
                plan_ref,
            ],
            smem,
            lists + (embedding, w_send, w_radial, w_update),
            12,
        )
        s2 = flat(padded(grid_of(s2_own), 1))
        g2, dh2, ds, listed, wide_rel = call(
            functools.partial(second_kernel, home),
            [
                shaped(blocks, bf16),
                shaped(blocks, f32),
                shaped(ext_count, bf16),
                jax.ShapeDtypeStruct((chunks + 1, rows, FEATS + channels), bf16),
                jax.ShapeDtypeStruct((blocks, FEATS + channels, 3 * atoms), bf16),
            ],
            [
                pltpu.VMEM((blocks, FEATS + channels, spread), bf16),
                pltpu.VMEM((2, rows, spread), bf16),
                pltpu.VMEM((2, rows, 3 * atoms), f32),
                pltpu.VMEM((chunks + 1, rows, wide), bf16),
                pltpu.VMEM((ext_count, channels, atoms), f32),
                pltpu.VMEM((blocks, channels, max(wide, spread)), f32),
                pltpu.VMEM((blocks, wide, channels), bf16),
                pltpu.VMEM((2, rows, channels), bf16),
                plan_ref,
            ],
            smem,
            lists + (s2, h1, w_radial, w_update, w_out, energy),
            40,
        )
        ds_own = flat(folded(ds.reshape(ext_shape + ds.shape[1:]), (grid_x, grid_y, grid_z), 2))
        (grad,) = call(
            functools.partial(third_kernel, home),
            [jax.ShapeDtypeStruct((ext_count, 8, atoms), f32)],
            [
                pltpu.VMEM((2, rows, spread), bf16),
                pltpu.VMEM((2, rows, 3 * atoms), f32),
                pltpu.VMEM((blocks, FEATS + channels, wide), bf16),
                pltpu.VMEM((2, rows, wide), f32),
                pltpu.VMEM((2, rows, 3 * atoms), bf16),
                pltpu.VMEM((2, 16, rows), bf16),
                pltpu.VMEM((blocks, 16, spread), f32),
                pltpu.VMEM((blocks, 24, atoms), f32),
                plan_ref,
            ],
            smem,
            (pos, dest, wide_rel, listed, g2, dh2, ds_own, u1, embedding, w_send, w_radial, w_update),
            14,
        )
        return grad.reshape(ext_shape + grad.shape[1:])

    def turned(value):
        return jnp.swapaxes(value, 2, 3)

    slot_total = (
        positions.size // 3 * lax.axis_size("gx") * lax.axis_size("gy") * lax.axis_size("gz")
    )
    positions, velocities = turned(positions), turned(velocities)
    pos = started(positions, species, 0)
    half, travelled, pos = kicked(gradient(flat(pos)), positions, velocities, species, masses, 3)
    speeds = thermostat(gradient(flat(pos)), half, species, masses, slot_total, 4)
    return (turned(travelled), turned(speeds))


def solution(mesh):
    placed = (
        P("gx", "gy", "gz", None, None),
        P("gx", "gy", "gz", None, None),
        P("gx", "gy", "gz", None),
        P("gx", "gy", "gz", None),
        P(),
        P(),
        P(),
        P(),
        P(),
        P(),
        P(),
    )
    return jax.shard_map(
        local,
        mesh=mesh,
        in_specs=placed,
        out_specs=(P("gx", "gy", "gz", None, None), P("gx", "gy", "gz", None, None)),
        check_vma=False,
    )
```

```python
import functools
import math

import jax
import jax.numpy as jnp
from jax import lax
from jax.experimental import pallas as pl
from jax.experimental.pallas import tpu as pltpu
from jax.sharding import PartitionSpec as P

soft_sq = 0.25
cut_sq = 25.0
gamma_width = 2.56
time_step = 1.0
target_slot = 0.25
tiny_eps = 1e-06
LOG2E = math.log2(math.e)
CHUNK = 32
bf16 = jnp.bfloat16
f32 = jnp.float32

SIDES = (("gx", 0), ("gy", 1), ("gz", 2))


MESH = pl.DeviceIdType.MESH


DIRECTIONS = [
    (dx, dy, dz) for dx in (-1, 0, 1) for dy in (-1, 0, 1) for dz in (-1, 0, 1) if dx or dy or dz
]


def around(direction):
    present, place = True, {}
    for (axis, _), step in zip(SIDES, direction):
        if step:
            there = lax.axis_index(axis) + step
            present = present & (there >= 0) & (there < lax.axis_size(axis))
            place[axis] = there
    return present, place


def opposite(direction):
    return tuple(-step for step in direction)


def greet(more=()):
    barrier = pltpu.get_barrier_semaphore()
    expected = len(more)
    for place in more:
        pl.semaphore_signal(barrier, inc=1, device_id=place, device_id_type=MESH)
    for direction in DIRECTIONS:
        present, place = around(direction)

        @pl.when(present)
        def _(place=place):
            pl.semaphore_signal(barrier, inc=1, device_id=place, device_id_type=MESH)

        expected = expected + present.astype(jnp.int32)
    return lambda: pl.semaphore_wait(barrier, expected)


def sent(direction, sizes):
    own, ext = [], []
    for step, size in zip(direction, sizes):
        own.append(pl.ds(0, size) if step == 0 else pl.ds(0 if step < 0 else size - 1, 1))
        ext.append(pl.ds(1, size) if step == 0 else pl.ds(size + 1 if step < 0 else 0, 1))
    return tuple(own), tuple(ext)


def rim(direction, sizes):
    return tuple(
        pl.ds(1, size) if step == 0 else pl.ds(0 if step < 0 else size + 1, 1)
        for step, size in zip(direction, sizes)
    )


def exchange(pairs, send_sem, recv_sem):
    copies = []
    for at, (direction, (source, target)) in enumerate(zip(DIRECTIONS, pairs)):
        present, place = around(direction)
        copy = pltpu.make_async_remote_copy(
            src_ref=source,
            dst_ref=target,
            send_sem=send_sem.at[at],
            recv_sem=recv_sem.at[at],
            device_id=place,
            device_id_type=MESH,
        )
        pl.when(present)(copy.start)
        copies.append((copy, present, around(opposite(direction))[0]))

    def finish():
        for copy, _, arrives in copies:
            pl.when(arrives)(copy.wait_recv)
        for copy, present, _ in copies:
            pl.when(present)(copy.wait_send)

    return finish


def blank_rim(ext, sizes):
    for direction in DIRECTIONS:

        @pl.when(jnp.logical_not(around(direction)[0]))
        def _(direction=direction):
            index = rim(direction, sizes)
            ext[index] = jnp.zeros(tuple(part.size for part in index) + ext.shape[3:], ext.dtype)


def spread_rim(own, ext, sizes, send_sem, recv_sem):
    pairs = []
    for direction in DIRECTIONS:
        mine, theirs = sent(direction, sizes)
        pairs.append((own.at[mine], ext.at[theirs]))
    return exchange(pairs, send_sem, recv_sem)


def halo_kernel(own, ext, send_sem, recv_sem, copy_sem):
    ready = greet()
    sizes = own.shape[:3]
    fill = pltpu.make_async_copy(own, ext.at[tuple(pl.ds(1, size) for size in sizes)], copy_sem)
    fill.start()
    blank_rim(ext, sizes)
    ready()
    finish = spread_rim(own, ext, sizes, send_sem, recv_sem)
    fill.wait()
    finish()


def start_kernel(positions, species, ext, send_sem, recv_sem, copy_sem, fresh):
    sizes = fresh.shape[:3]
    for x, y, z in cells_of(sizes):
        rows = [positions[x, y, d, z : z + 1, :] for d in range(3)]
        fresh[x, y, z] = tile_of(rows + [species[x, y, z : z + 1, :].astype(f32)])
    halo_kernel(fresh, ext, send_sem, recv_sem, copy_sem)


def tile_of(rows):
    row = lax.broadcasted_iota(jnp.int32, (8, rows[0].shape[-1]), 0)
    tile = jnp.zeros(row.shape, f32)
    for at, value in enumerate(rows):
        tile = jnp.where(row == at, value, tile)
    return tile


def mass_of(species, masses):
    mass = jnp.full(species.shape, masses[0], f32)
    for kind in range(1, masses.shape[0]):
        mass = jnp.where(species == kind, masses[kind], mass)
    return mass


def landing_scratch(sizes, tail, dtype):
    return [
        pltpu.VMEM(tuple(1 if step else size for step, size in zip(direction, sizes)) + tail, dtype)
        for direction in DIRECTIONS
    ]


def blank_lands(lands):
    for direction, land in zip(DIRECTIONS, lands):

        @pl.when(jnp.logical_not(around(opposite(direction))[0]))
        def _(land=land):
            land[...] = jnp.zeros_like(land)


def gather_rim(ext, lands, sizes, send_sem, recv_sem):
    pairs = [(ext.at[rim(direction, sizes)], land) for direction, land in zip(DIRECTIONS, lands)]
    return exchange(pairs, send_sem, recv_sem)


def cells_of(sizes):
    return [(x, y, z) for x in range(sizes[0]) for y in range(sizes[1]) for z in range(sizes[2])]


def landed(ext, lands, sizes, cell):
    value = ext[tuple(at + 1 for at in cell)].astype(f32)
    for direction, land in zip(DIRECTIONS, lands):
        index = []
        for step, size, at in zip(direction, sizes, cell):
            if step == 0:
                index.append(at)
            elif at == (size - 1 if step < 0 else 0):
                index.append(0)
        if len(index) == 3:
            value = value + land[tuple(index)].astype(f32)
    return value


def fold_kernel(ext, own, *refs):
    lands, (send_sem, recv_sem) = refs[:26], refs[26:]
    ready = greet()
    sizes = own.shape[:3]
    blank_lands(lands)
    ready()
    gather_rim(ext, lands, sizes, send_sem, recv_sem)()
    for cell in cells_of(sizes):
        own[cell] = landed(ext, lands, sizes, cell).astype(own.dtype)


def kick_kernel(masses, ext, positions, velocities, species, out_half, out_moved, out_pos, *refs):
    lands, (send_sem, recv_sem, send_two, recv_two, copy_sem, fresh) = refs[:26], refs[26:]
    ready = greet()
    sizes = fresh.shape[:3]
    blank_lands(lands)
    blank_rim(out_pos, sizes)
    ready()
    gather_rim(ext, lands, sizes, send_sem, recv_sem)()
    for cell in cells_of(sizes):
        x, y, z = cell
        kinds = species[x, y, z : z + 1, :]
        force = -landed(ext, lands, sizes, cell) * (0.5 * time_step / mass_of(kinds, masses))
        rows = []
        for d in range(3):
            half_kick = velocities[x, y, d, z : z + 1, :] + force[d : d + 1, :]
            moved = time_step * half_kick
            out_half[x, y, d, z : z + 1, :] = half_kick
            out_moved[x, y, d, z : z + 1, :] = moved
            rows.append(positions[x, y, d, z : z + 1, :] + moved)
        fresh[cell] = tile_of(rows + [kinds.astype(f32)])
    fill = pltpu.make_async_copy(fresh, out_pos.at[tuple(pl.ds(1, size) for size in sizes)], copy_sem)
    fill.start()
    finish = spread_rim(fresh, out_pos, sizes, send_two, recv_two)
    fill.wait()
    finish()


def ring(axes):
    steps = [()]
    for axis in axes:
        steps = [step + (t,) for step in steps for t in range(lax.axis_size(axis))]
    places = []
    for step in steps[1:]:
        places.append(
            {axis: lax.rem(lax.axis_index(axis) + t, lax.axis_size(axis)) for axis, t in zip(axes, step) if t}
        )
    return places


STAGES = (("gx", "gy"), ("gz",))


def last_kernel(slot_total, masses, ext, half, species, out, *refs):
    lands, refs = refs[:26], refs[26:]
    send_sem, recv_sem, send_two, recv_two, speed = refs[:5]
    inbox, sums = refs[5:7], refs[7:9]
    ready = greet([place for axes in STAGES for place in ring(axes)])
    sizes = speed.shape[:3]
    blank_lands(lands)
    ready()
    gather_rim(ext, lands, sizes, send_sem, recv_sem)()
    total = jnp.zeros(speed.shape[3:], f32)
    for cell in cells_of(sizes):
        x, y, z = cell
        kinds = species[x, y, z : z + 1, :]
        mass = mass_of(kinds, masses)
        force = -landed(ext, lands, sizes, cell) * (0.5 * time_step / mass)
        velocity = tile_of([half[x, y, d, z : z + 1, :] + force[d : d + 1, :] for d in range(3)])
        speed[cell] = velocity
        total = total + jnp.where(kinds > 0, 0.5 * mass, 0.0) * velocity * velocity
    base = 0
    for stage, axes in enumerate(STAGES):
        sums[stage][...] = total
        copies = []
        for t, place in enumerate(ring(axes)):
            copy = pltpu.make_async_remote_copy(
                src_ref=sums[stage],
                dst_ref=inbox[stage].at[t],
                send_sem=send_two.at[base],
                recv_sem=recv_two.at[base],
                device_id=place,
                device_id_type=MESH,
            )
            copy.start()
            copies.append(copy)
            base += 1
        for t, copy in enumerate(copies):
            copy.wait()
            total = total + inbox[stage][t]
    kinetic = jnp.sum(total, keepdims=True)
    factor = jnp.sqrt(target_slot * slot_total / (kinetic + tiny_eps))
    for x, y, z in cells_of(sizes):
        value = speed[x, y, z] * factor
        for d in range(3):
            out[x, y, d, z : z + 1, :] = value[d : d + 1, :]


def vmem_specs(count):
    return [pl.BlockSpec(memory_space=pltpu.VMEM)] * count


def remote_call(kernel, outs, scratch, collective_id, args, smem=()):
    return pl.pallas_call(
        kernel,
        out_shape=outs,
        in_specs=[pl.BlockSpec(memory_space=pltpu.SMEM)] * len(smem) + vmem_specs(len(args)),
        out_specs=vmem_specs(len(outs)),
        scratch_shapes=scratch,
        compiler_params=pltpu.CompilerParams(
            collective_id=collective_id, has_side_effects=True, vmem_limit_bytes=5 << 20
        ),
    )(*smem, *args)


def semaphores():
    return [pltpu.SemaphoreType.DMA((26,)), pltpu.SemaphoreType.DMA((26,))]


def padded_shape(shape, dtype):
    return jax.ShapeDtypeStruct(tuple(size + 2 for size in shape[:3]) + shape[3:], dtype)


def padded(cells, collective_id):
    scratch = semaphores() + [pltpu.SemaphoreType.DMA]
    return remote_call(halo_kernel, [padded_shape(cells.shape, cells.dtype)], scratch, collective_id, (cells,))[0]


def tiles_shape(species):
    return species.shape[:3] + (8,) + species.shape[3:]


def started(positions, species, collective_id):
    tiles = tiles_shape(species)
    scratch = semaphores() + [pltpu.SemaphoreType.DMA, pltpu.VMEM(tiles, f32)]
    return remote_call(start_kernel, [padded_shape(tiles, f32)], scratch, collective_id, (positions, species))[0]


def folded(grid, sizes, collective_id):
    tail = grid.shape[3:]
    scratch = landing_scratch(sizes, tail, grid.dtype) + semaphores()
    out = jax.ShapeDtypeStruct(sizes + tail, grid.dtype)
    return remote_call(fold_kernel, [out], scratch, collective_id, (grid,))[0]


def kicked(grid, positions, velocities, species, masses, collective_id):
    tiles = tiles_shape(species)
    scratch = landing_scratch(tiles[:3], tiles[3:], f32) + semaphores() + semaphores()
    scratch += [pltpu.SemaphoreType.DMA, pltpu.VMEM(tiles, f32)]
    raw = jax.ShapeDtypeStruct(positions.shape, f32)
    outs = [raw, raw, padded_shape(tiles, f32)]
    return remote_call(kick_kernel, outs, scratch, collective_id, (grid, positions, velocities, species), (masses,))


def thermostat(grid, half, species, masses, slot_total, collective_id):
    tiles = tiles_shape(species)
    counts = [math.prod(lax.axis_size(axis) for axis in axes) for axes in STAGES]
    peers = sum(count - 1 for count in counts)
    scratch = landing_scratch(tiles[:3], tiles[3:], f32) + semaphores()
    scratch += [pltpu.SemaphoreType.DMA((peers,)), pltpu.SemaphoreType.DMA((peers,)), pltpu.VMEM(tiles, f32)]
    scratch += [pltpu.VMEM((max(count - 1, 1),) + tiles[3:], f32) for count in counts]
    scratch += [pltpu.VMEM(tiles[3:], f32)] * 2
    out = jax.ShapeDtypeStruct(half.shape, f32)
    kernel = functools.partial(last_kernel, float(slot_total))
    return remote_call(kernel, [out], scratch, collective_id, (grid, half, species), (masses,))[0]


def slot_tables(neighbour_blocks):
    size_x, size_y, size_z, slot_count = neighbour_blocks.shape
    is_live = neighbour_blocks < 27
    offset = jnp.where(is_live, neighbour_blocks, 13)
    index_x = lax.broadcasted_iota(jnp.int32, neighbour_blocks.shape, 0)
    index_y = lax.broadcasted_iota(jnp.int32, neighbour_blocks.shape, 1)
    index_z = lax.broadcasted_iota(jnp.int32, neighbour_blocks.shape, 2)
    source = (
        (index_x + offset // 9) * (size_y + 2) + (index_y + offset // 3 % 3)
    ) * (size_z + 2) + (index_z + offset % 3)
    return source.reshape(-1, slot_count)


def basis_constants(basis_count):
    step = 5.0 / basis_count
    mid = basis_count // 2
    centers = [(k + 0.5) * step for k in range(basis_count)]
    scales = [math.exp(-gamma_width * (centers[k] - centers[mid]) ** 2) for k in range(basis_count)]
    return step, mid, centers, scales


def geometry(apart, row0, basis_count):
    step, mid, centers, _ = basis_constants(basis_count)
    atoms = apart.shape[1] // 3
    rows = slice(row0, row0 + CHUNK)
    steps = [apart[rows, d * atoms : (d + 1) * atoms] for d in range(3)]
    dx, dy, dz = steps
    squared = jnp.minimum(dx * dx + dy * dy + dz * dz, cut_sq)
    cut = 1.0 - squared * (1.0 / cut_sq)
    soft = squared + soft_sq
    inv = lax.rsqrt(soft)
    shift = soft * inv - centers[mid]
    bell = jnp.exp2((-gamma_width * LOG2E) * (shift * shift))
    slope = shift * (2.0 * gamma_width * step * LOG2E)
    return steps, cut, inv, bell, jnp.exp2(slope), jnp.exp2(-slope)


def radial_powers(start, up, down, basis_count):
    mid = basis_count // 2
    powers = [None] * basis_count
    powers[mid] = start
    for k in range(mid + 1, basis_count):
        powers[k] = powers[k - 1] * up
    for k in range(mid - 1, -1, -1):
        powers[k] = powers[k + 1] * down
    scales = basis_constants(basis_count)[3]
    return [power * scale if scale != 1.0 else power for power, scale in zip(powers, scales)]


def fill_kernel(store, apart, c, basis_count):
    rows, atoms = apart.shape[0], apart.shape[1] // 3
    for row0 in range(0, rows, CHUNK):
        _, cut, _, bell, up, down = geometry(apart, row0, basis_count)
        ahead = lax.broadcasted_iota(jnp.int32, cut.shape, 1) - lax.broadcasted_iota(jnp.int32, cut.shape, 0)
        cut = jnp.where(ahead == row0 + c * rows, 0.0, cut)
        for k, value in enumerate(radial_powers(cut * cut * bell, up, down, basis_count)):
            store[row0 : row0 + CHUNK, k * atoms : (k + 1) * atoms] = value.astype(bf16)


def split(value):
    high = value.astype(bf16)
    return high, (value - high.astype(f32)).astype(bf16)


def dot_split(a, value):
    high, low = split(value)
    return dot(a, high) + dot(a, low)


def held(value):
    return value.astype(bf16).astype(f32)


def narrowed(radial, sums):
    atoms = radial[0].shape[-1]
    return sum(column * sums[:, k * atoms : (k + 1) * atoms] for k, column in enumerate(radial))


def silu_grad(value):
    gate = jax.nn.sigmoid(value)
    return gate * (1.0 + value * (1.0 - gate))


def dot(a, b):
    return jnp.dot(a, b, preferred_element_type=f32)


def dot_wide(a, b):
    return jnp.dot(a, b, preferred_element_type=f32, precision=lax.Precision.HIGHEST)


def dot_nt(a, b):
    return lax.dot_general(a, b, (((1,), (1,)), ((), ())), preferred_element_type=f32)


def dot_tn(a, b):
    return lax.dot_general(a, b, (((0,), (0,)), ((), ())), preferred_element_type=f32)


FEATS = 32


def thirds(value):
    high = held(value)
    rest = value - high
    mid = held(rest)
    return high, mid, rest - mid


def side(values):
    return jnp.concatenate(values, axis=1)


def features(block, origin):
    row = lax.broadcasted_iota(jnp.int32, block.shape, 0)
    where = jnp.where(row < 3, block - origin, 0.0)
    square = jnp.sum(where * where, axis=0, keepdims=True) * near_part
    high = held(square)
    tiles = [jnp.where(row < 3, part, jnp.where(row == 3, 1.0, 0.0)) for part in thirds(where)]
    again = pltpu.roll(jnp.where(row < 3, tiles[0], 0.0), 4, 0)
    kinds = jnp.where((row > 3) & (block[3:4, :] == row.astype(f32) - 4.0), 1.0, 0.0)
    tiles[0] = jnp.where(row > 3, kinds, tiles[0])
    tiles[1] = jnp.where(row == 4, high, jnp.where(row == 5, square - high, tiles[1]))
    tiles[2] = tiles[2] + again
    return jnp.concatenate(tiles + [kinds], axis=0).astype(bf16)


near_part = 1.0 - 2.0**-13


def reach_rows(own, origin):
    row = lax.broadcasted_iota(jnp.int32, own.shape, 0)
    where = jnp.where(row < 3, own - origin, 0.0)
    square = jnp.sum(where * where, axis=0, keepdims=True) * near_part
    square = jnp.where(own[3:4, :] > 0.0, square, 1e9)
    top = held(square)
    high, mid, _ = thirds(where)
    tiles = [
        jnp.where(row == 3, top, -2.0 * high),
        jnp.where(row == 3, square - top, jnp.where((row == 4) | (row == 5), 1.0, -2.0 * high)),
        pltpu.roll(-2.0 * mid, 4, 0),
        jnp.zeros_like(own),
    ]
    return jnp.concatenate(tiles, axis=0).astype(bf16)


def set_apart(rel, own, origin):
    atoms = own.shape[-1]
    row = lax.broadcasted_iota(jnp.int32, (FEATS, atoms), 0)
    high, mid, low = thirds(own - origin)
    for d in range(3):
        tile = jnp.where((row == d) | (row == 8 + d) | (row == 16 + d), 1.0, 0.0)
        for at, part in ((3, high), (11, mid), (19, low)):
            tile = jnp.where(row == at, -part[d : d + 1, :], tile)
        rel[:, d * atoms : (d + 1) * atoms] = tile.astype(bf16)


def list_kernel(home, src, pos, dest, count, table, rel, hits):
    blocks, slots = src.shape
    atoms = pos.shape[-1]
    origin = pos[home[0]][:, 0:1]
    for b in range(blocks):
        own = pos[home[b]]
        set_apart(rel.at[b], own, origin)
        for q in range(slots):
            table[b, :, q * atoms : (q + 1) * atoms] = features(pos[src[b, q]], origin)
    for b in range(blocks):
        reach = dot_tn(reach_rows(pos[home[b]], origin), table[b])
        reach = jnp.min(reach, axis=0, keepdims=True)
        for q in range(slots):
            live = 1.0 if q == 0 else (src[b, q] != home[b]).astype(f32)
            real = pos[src[b, q]][3:4, :] > 0.0
            near = (reach[:, q * atoms : (q + 1) * atoms] < cut_sq * 1.001) & real
            hits[b * slots + q : b * slots + q + 1, :] = jnp.where(near, live, 0.0)
    hit = hits[...]
    shape = (atoms, atoms)
    upto = lax.broadcasted_iota(jnp.int32, shape, 0) <= lax.broadcasted_iota(jnp.int32, shape, 1)
    inside = dot(hit.astype(bf16), jnp.where(upto, 1.0, 0.0).astype(bf16))
    total = jnp.broadcast_to(inside[:, atoms - 1 : atoms], hit.shape)
    pairs = blocks * slots
    r0 = lax.broadcasted_iota(jnp.int32, (pairs, pairs), 0)
    r1 = lax.broadcasted_iota(jnp.int32, (pairs, pairs), 1)
    group0 = jnp.floor((r0.astype(f32) + 0.5) * (1.0 / slots))
    group1 = jnp.floor((r1.astype(f32) + 0.5) * (1.0 / slots))
    before = jnp.where((group0 == group1) & (r1 < r0), 1.0, 0.0).astype(bf16)
    start = dot(before, total.astype(bf16))
    dest[...] = jnp.where(hit > 0.0, start + inside - 1.0, -1.0).astype(jnp.int32)
    line = lax.broadcasted_iota(jnp.int32, hit.shape, 0)
    lane = lax.broadcasted_iota(jnp.int32, hit.shape, 1)
    last = jnp.where(line == lane * slots + (slots - 1), start + total, 0.0)
    count[...] = jnp.sum(last, axis=0, keepdims=True).astype(jnp.int32)


def set_places(place, dest, b, c):
    rows, atoms = place.shape[0], dest.shape[1]
    slots = place.shape[1] // atoms
    to = dest[pl.ds(pl.multiple_of(b * slots, slots), slots), :]
    to = jnp.clip(to - c * rows, -1, rows).astype(f32)
    row = lax.broadcasted_iota(jnp.int32, (rows, atoms), 0).astype(f32).astype(bf16)
    one, none = jnp.ones((rows, atoms), bf16), jnp.zeros((rows, atoms), bf16)
    for q in range(slots):
        here = jnp.broadcast_to(to[q : q + 1, :], (rows, atoms)).astype(bf16)
        place[:, q * atoms : (q + 1) * atoms] = jnp.where(here == row, one, none)


def plan(count, plan_ref, blocks, rows):
    def of_block(b, n):
        chunks = jnp.maximum(count[0, b] + (rows - 1), rows) // rows

        def of_chunk(c, n):
            plan_ref[0, n] = b
            plan_ref[1, n] = c
            return n + 1

        return lax.fori_loop(0, chunks, of_chunk, n)

    return lax.fori_loop(0, blocks, of_block, 0)


def pipelined(total, plan_ref, stages):
    last = len(stages) - 1

    def run(t, chosen):
        for s in reversed(chosen):
            n = t - s
            stages[s](n, plan_ref[0, n], plan_ref[1, n])

    def step(t, carry):
        run(t, range(last + 1))
        return carry

    for t in range(last):
        run(t, range(t + 1))
    lax.fori_loop(last, total, step, 0)
    for t in range(last):
        run(total + t, range(t + 1, last + 1))


def mix_rows(embedding, w_send, w_radial):
    kinds, channels = embedding.shape
    rows = dot(embedding[...], w_send[0]).astype(bf16).astype(f32)
    row = lax.broadcasted_iota(jnp.int32, (8, channels), 0)
    tile = jnp.zeros((8, channels), f32)
    for kind in range(1, kinds):
        tile = jnp.where(row == 4 + kind, rows[kind : kind + 1, :], tile)
    return jnp.concatenate([tile * w_radial[0, k : k + 1, :] for k in range(w_radial.shape[1])], axis=0)


def columns(rows, atoms):
    turned = rows.T
    return [jnp.broadcast_to(turned[:, k : k + 1], (turned.shape[0], atoms)) for k in range(rows.shape[0])]


def first_kernel(home, src, count, pos, dest, table, rel, embedding, w_send, w_radial, w_update,
                 h1_out, u1_out, s2_out, listed, place, apart, store, sums, stack, plan_ref):
    blocks, slots = src.shape
    atoms = pos.shape[-1]
    basis_count = store.shape[2] // atoms
    total = plan(count, plan_ref, blocks, store.shape[1])
    sums[...] = jnp.zeros_like(sums)

    def places(n, b, c):
        set_places(place.at[n & 1], dest, b, c)

    def gather(n, b, c):
        listed[n & 3] = dot_nt(place[n & 1], table[b]).astype(bf16)

    def differ(n, b, c):
        apart[n & 1] = dot(listed[n & 3], rel[b])

    def fill(n, b, c):
        fill_kernel(store.at[n & 1], apart.at[n & 1], c, basis_count)

    def collect(n, b, c):
        sums[b] += dot_tn(listed[n & 3][:, :8], store[n & 1])

    pipelined(total, plan_ref, [places, gather, differ, fill, collect])
    row = lax.broadcasted_iota(jnp.int32, (embedding.shape[0], atoms), 0).astype(f32)
    species = [pos[home[b]][3:4, :] for b in range(blocks)]
    kinds = side([jnp.where(row == one, 1.0, 0.0) for one in species]).astype(bf16)
    for b in range(blocks):
        for k in range(basis_count):
            stack[k * 8 : (k + 1) * 8, b * atoms : (b + 1) * atoms] = sums[b, :, k * atoms : (k + 1) * atoms]
    mix = mix_rows(embedding, w_send, w_radial)
    message = lax.dot_general(
        mix, stack[...], (((0,), (0,)), ((), ())), preferred_element_type=f32, precision=lax.Precision.HIGHEST
    )
    update = dot_tn(w_update[0], message.astype(bf16))
    hidden = (dot_tn(embedding[...], kinds) + update * jax.nn.sigmoid(update)).astype(bf16)
    sender = jnp.where(side(species) > 0.0, dot_tn(w_send[1], hidden), 0.0).astype(bf16)
    for b in range(blocks):
        there = slice(b * atoms, (b + 1) * atoms)
        h1_out[b] = hidden[:, there]
        u1_out[b] = update[:, there]
        s2_out[b] = sender[:, there]


def set_table(full, table, s2, src):
    blocks, slots = src.shape
    atoms = s2.shape[2]
    channels = s2.shape[1]
    full[:, channels:, :] = table[...]
    for b in range(blocks):
        for q in range(slots):
            full[b, :channels, q * atoms : (q + 1) * atoms] = s2[src[b, q]]


def second_kernel(home, src, count, pos, dest, table, rel, s2, h1, w_radial, w_update, w_out,
                  energy, g2_out, dh2_out, ds_out, listed, wide_rel, full, place, apart, store, acc, sums, wide,
                  both, plan_ref):
    blocks, slots = src.shape
    channels, atoms = s2.shape[1:]
    basis_count = w_radial.shape[1]
    total = plan(count, plan_ref, blocks, store.shape[1])
    set_table(full, table, s2, src)
    wide_rel[:, :channels, :] = jnp.zeros((blocks, channels, rel.shape[2]), bf16)
    wide_rel[:, channels:, :] = rel[...]
    sums[...] = jnp.zeros_like(sums)

    def places(n, b, c):
        set_places(place.at[n & 1], dest, b, c)

    def gather(n, b, c):
        listed[n] = dot_nt(place[n & 1], full[b]).astype(bf16)

    def differ(n, b, c):
        apart[n & 1] = dot(listed[n], wide_rel[b])

    def fill(n, b, c):
        fill_kernel(store.at[n], apart.at[n & 1], c, basis_count)

    def collect(n, b, c):
        sums[b] += dot_tn(listed[n][:, :channels], store[n])

    pipelined(total, plan_ref, [places, gather, differ, fill, collect])
    radial = columns(w_radial[1], atoms)
    message = side([narrowed(radial, sums.at[b]) for b in range(blocks)])
    up = dot_tn(w_update[1], message.astype(bf16))
    second = side([h1[b] for b in range(blocks)]).astype(f32) + up * jax.nn.sigmoid(up)
    hidden = dot_tn(w_out[...], second.astype(bf16))
    real = side([pos[home[b]][3:4, :] for b in range(blocks)]) > 0.0
    d_hidden = jnp.where(real, columns(energy[...], blocks * atoms)[0] * silu_grad(hidden), 0.0)
    d_second = held(dot_split(w_out[...], d_hidden))
    g2 = dot_split(w_update[1], d_second * silu_grad(up)).astype(bf16)
    for b in range(blocks):
        there = slice(b * atoms, (b + 1) * atoms)
        dh2_out[b] = d_second[:, there]
        g2_out[b] = g2[:, there]
        turned = g2[:, there].astype(f32).T
        for k in range(basis_count):
            wide[b, k * atoms : (k + 1) * atoms, :] = (turned * w_radial[1, k : k + 1, :]).astype(bf16)
    sums[...] = jnp.zeros_like(sums)

    def project(n, b, c):
        both[n & 1] = dot(store[n], wide[b]).astype(bf16)
        set_places(place.at[n & 1], dest, b, c)

    def scatter(n, b, c):
        sums[b] += dot_tn(both[n & 1], place[n & 1])

    pipelined(total, plan_ref, [project, scatter])
    acc[...] = jnp.zeros_like(acc)
    for b in range(blocks):
        for q in range(slots):
            acc[src[b, q]] += sums[b, :, q * atoms : (q + 1) * atoms]
    ds_out[...] = acc[...].astype(bf16)


def third_kernel(home, src, count, pos, dest, rel, listed, g2, dh2, ds, u1, embedding, w_send, w_radial, w_update,
                 grad_out, place, apart, wide, parts, pulls, turned, back, pull, plan_ref):
    blocks, slots = src.shape
    channels, atoms = g2.shape[1:]
    rows = parts.shape[1]
    basis_count = w_radial.shape[1]
    _, _, centers, _ = basis_constants(basis_count)
    total = plan(count, plan_ref, blocks, rows)
    row16 = lax.broadcasted_iota(jnp.int32, (16, rows), 0)
    unit = lax.broadcasted_iota(jnp.int32, (16, atoms), 0)
    folds = side([jnp.where((unit == d) | (unit == 8 + d), 1.0, 0.0) for d in range(3)]).astype(bf16)
    real = side([pos[home[b]][3:4, :] for b in range(blocks)]) > 0.0

    def joined(ref):
        return side([ref[b] for b in range(blocks)])

    dh1 = held(joined(dh2) + dot(w_send[1], joined(ds)))
    du1 = dh1 * silu_grad(joined(u1))
    g1 = jnp.where(real, dot_split(w_update[0], du1), 0.0)
    by_kind = dot_wide(mix_rows(embedding, w_send, w_radial), g1)
    radial = columns(w_radial[1], atoms)
    blank = jnp.zeros((FEATS - 16, atoms), f32)
    for b in range(blocks):
        g2_here = g2[b].astype(f32)
        for k in range(basis_count):
            there = slice(k * atoms, (k + 1) * atoms)
            first = by_kind[k * 8 : (k + 1) * 8, b * atoms : (b + 1) * atoms]
            high = held(first)
            wide[b, channels:, there] = jnp.concatenate([high, blank, first - high], axis=0).astype(bf16)
            wide[b, :channels, there] = (radial[k] * g2_here).astype(bf16)
    back[...] = jnp.zeros_like(back)
    pull[...] = jnp.zeros_like(pull)

    def differ(n, b, c):
        apart[n & 1] = dot(listed[n], rel[b])
        parts[n & 1] = dot(listed[n], wide[b])

    def pair(n, b, c):
        sides = [jnp.zeros((8, atoms), f32)] * 3
        for row0 in range(0, rows, CHUNK):
            steps, cut, inv, bell, up, down = geometry(apart.at[n & 1], row0, basis_count)
            plain = jnp.zeros_like(cut)
            moment = jnp.zeros_like(cut)
            for k, value in enumerate(radial_powers(bell, up, down, basis_count)):
                term = value * parts[n & 1, row0 : row0 + CHUNK, k * atoms : (k + 1) * atoms]
                plain = plain + term
                moment = moment + centers[k] * term
            scaled = gamma_width * cut
            size = cut * (moment * (scaled * inv) - plain * (scaled + 2.0 / cut_sq))
            for d in range(3):
                force = size * steps[d]
                pulls[n & 1, row0 : row0 + CHUNK, d * atoms : (d + 1) * atoms] = force.astype(bf16)
                sides[d] = sides[d] + jnp.sum(force.reshape(CHUNK // 8, 8, atoms), axis=0)
        pull[b] += jnp.concatenate(sides, axis=0)

    def turn(n, b, c):
        value = dot_nt(folds, pulls[n & 1])
        high = held(value)
        turned[n & 1] = jnp.where(row16 < 8, high, value - high).astype(bf16)
        set_places(place.at[n & 1], dest, b, c)

    def scatter(n, b, c):
        back[b] += dot(turned[n & 1], place[n & 1])

    pipelined(total, plan_ref, [differ, pair, turn, scatter])
    grad_out[...] = jnp.zeros_like(grad_out)
    row8 = lax.broadcasted_iota(jnp.int32, (8, atoms), 0)
    for b in range(blocks):
        for q in range(slots):
            there = slice(q * atoms, (q + 1) * atoms)
            grad_out[src[b, q]] += 2.0 * (back[b, :8, there] + back[b, 8:, there])
        for d in range(3):
            at_target = jnp.sum(pull[b, d * 8 : (d + 1) * 8, :], axis=0, keepdims=True)
            grad_out[home[b]] -= jnp.where(row8 == d, 2.0 * at_target, 0.0)


def call(kernel, outs, scratch, smem, args, limit):
    return pl.pallas_call(
        kernel,
        out_shape=outs,
        in_specs=[pl.BlockSpec(memory_space=pltpu.SMEM)] * len(smem)
        + [pl.BlockSpec(memory_space=pltpu.VMEM)] * len(args),
        out_specs=[pl.BlockSpec(memory_space=pltpu.VMEM)] * len(outs),
        scratch_shapes=scratch,
        compiler_params=pltpu.CompilerParams(vmem_limit_bytes=limit << 20),
    )(*smem, *args)


def local(
    positions,
    velocities,
    species,
    neighbour_blocks,
    embedding,
    w_send,
    w_radial,
    w_update,
    w_out,
    w_energy,
    masses,
):
    grid_x, grid_y, grid_z = positions.shape[:3]
    atoms = positions.shape[-1]
    channels = w_send.shape[-1]
    basis_count = w_radial.shape[1]
    kinds = masses.shape[0]
    blocks = grid_x * grid_y * grid_z
    ext_shape = (grid_x + 2, grid_y + 2, grid_z + 2)
    ext_count = ext_shape[0] * ext_shape[1] * ext_shape[2]
    home = [
        ((x + 1) * ext_shape[1] + y + 1) * ext_shape[2] + z + 1
        for x in range(grid_x)
        for y in range(grid_y)
        for z in range(grid_z)
    ]
    src = slot_tables(neighbour_blocks)
    slots = src.shape[1]
    energy = w_energy[None, :]
    wide = basis_count * atoms
    spread = slots * atoms

    def shaped(count, dtype):
        return jax.ShapeDtypeStruct((count, channels, atoms), dtype)

    def grid_of(value):
        return value.reshape((grid_x, grid_y, grid_z) + value.shape[1:])

    def flat(value):
        return value.reshape((-1,) + value.shape[3:])

    def gradient(pos):
        dest, count, table, rel = call(
            functools.partial(list_kernel, home),
            [
                jax.ShapeDtypeStruct((blocks * slots, atoms), jnp.int32),
                jax.ShapeDtypeStruct((1, atoms), jnp.int32),
                jax.ShapeDtypeStruct((blocks, FEATS, spread), bf16),
                jax.ShapeDtypeStruct((blocks, FEATS, 3 * atoms), bf16),
            ],
            [pltpu.VMEM((blocks * slots, atoms), f32)],
            (src,),
            (pos,),
            4,
        )
        smem = (src, count)
        lists = (pos, dest, table, rel)
        rows = atoms + atoms // 2
        chunks = blocks * (-(-slots * atoms // rows))
        plan_ref = pltpu.SMEM((2, chunks), jnp.int32)
        h1, u1, s2_own = call(
            functools.partial(first_kernel, home),
            [shaped(blocks, bf16), shaped(blocks, f32), shaped(blocks, bf16)],
            [
                pltpu.VMEM((4, rows, FEATS), bf16),
                pltpu.VMEM((2, rows, spread), bf16),
                pltpu.VMEM((2, rows, 3 * atoms), f32),
                pltpu.VMEM((2, rows, wide), bf16),
                pltpu.VMEM((blocks, 8, wide), f32),
                pltpu.VMEM((basis_count * 8, blocks * atoms), f32),
                plan_ref,
            ],
            smem,
            lists + (embedding, w_send, w_radial, w_update),
            7,
        )
        s2 = flat(padded(grid_of(s2_own), 1))
        g2, dh2, ds, listed, wide_rel = call(
            functools.partial(second_kernel, home),
            [
                shaped(blocks, bf16),
                shaped(blocks, f32),
                shaped(ext_count, bf16),
                jax.ShapeDtypeStruct((chunks, rows, FEATS + channels), bf16),
                jax.ShapeDtypeStruct((blocks, FEATS + channels, 3 * atoms), bf16),
            ],
            [
                pltpu.VMEM((blocks, FEATS + channels, spread), bf16),
                pltpu.VMEM((2, rows, spread), bf16),
                pltpu.VMEM((2, rows, 3 * atoms), f32),
                pltpu.VMEM((chunks, rows, wide), bf16),
                pltpu.VMEM((ext_count, channels, atoms), f32),
                pltpu.VMEM((blocks, channels, max(wide, spread)), f32),
                pltpu.VMEM((blocks, wide, channels), bf16),
                pltpu.VMEM((2, rows, channels), bf16),
                plan_ref,
            ],
            smem,
            lists + (s2, h1, w_radial, w_update, w_out, energy),
            36,
        )
        ds_own = flat(folded(ds.reshape(ext_shape + ds.shape[1:]), (grid_x, grid_y, grid_z), 2))
        (grad,) = call(
            functools.partial(third_kernel, home),
            [jax.ShapeDtypeStruct((ext_count, 8, atoms), f32)],
            [
                pltpu.VMEM((2, rows, spread), bf16),
                pltpu.VMEM((2, rows, 3 * atoms), f32),
                pltpu.VMEM((blocks, FEATS + channels, wide), bf16),
                pltpu.VMEM((2, rows, wide), f32),
                pltpu.VMEM((2, rows, 3 * atoms), bf16),
                pltpu.VMEM((2, 16, rows), bf16),
                pltpu.VMEM((blocks, 16, spread), f32),
                pltpu.VMEM((blocks, 24, atoms), f32),
                plan_ref,
            ],
            smem,
            (pos, dest, wide_rel, listed, g2, dh2, ds_own, u1, embedding, w_send, w_radial, w_update),
            11,
        )
        return grad.reshape(ext_shape + grad.shape[1:])

    def turned(value):
        return jnp.swapaxes(value, 2, 3)

    slot_total = (
        positions.size // 3 * lax.axis_size("gx") * lax.axis_size("gy") * lax.axis_size("gz")
    )
    positions, velocities = turned(positions), turned(velocities)
    pos = started(positions, species, 0)
    half, travelled, pos = kicked(gradient(flat(pos)), positions, velocities, species, masses, 3)
    speeds = thermostat(gradient(flat(pos)), half, species, masses, slot_total, 4)
    return (turned(travelled), turned(speeds))


def solution(mesh):
    placed = (
        P("gx", "gy", "gz", None, None),
        P("gx", "gy", "gz", None, None),
        P("gx", "gy", "gz", None),
        P("gx", "gy", "gz", None),
        P(),
        P(),
        P(),
        P(),
        P(),
        P(),
        P(),
    )
    return jax.shard_map(
        local,
        mesh=mesh,
        in_specs=placed,
        out_specs=(P("gx", "gy", "gz", None, None), P("gx", "gy", "gz", None, None)),
        check_vma=False,
    )
```

```python
import functools
import math

import jax
import jax.numpy as jnp
from jax import lax
from jax.experimental import pallas as pl
from jax.experimental.pallas import tpu as pltpu
from jax.sharding import PartitionSpec as P

soft_sq = 0.25
cut_sq = 25.0
gamma_width = 2.56
time_step = 1.0
target_slot = 0.25
tiny_eps = 1e-06
LOG2E = math.log2(math.e)
CHUNK = 16
bf16 = jnp.bfloat16
f32 = jnp.float32

SIDES = (("gx", 0), ("gy", 1), ("gz", 2))


MESH = pl.DeviceIdType.MESH


DIRECTIONS = [
    (dx, dy, dz) for dx in (-1, 0, 1) for dy in (-1, 0, 1) for dz in (-1, 0, 1) if dx or dy or dz
]


def around(direction):
    present, place = True, {}
    for (axis, _), step in zip(SIDES, direction):
        if step:
            there = lax.axis_index(axis) + step
            present = present & (there >= 0) & (there < lax.axis_size(axis))
            place[axis] = there
    return present, place


def opposite(direction):
    return tuple(-step for step in direction)


def greet(more=()):
    barrier = pltpu.get_barrier_semaphore()
    expected = len(more)
    for place in more:
        pl.semaphore_signal(barrier, inc=1, device_id=place, device_id_type=MESH)
    for direction in DIRECTIONS:
        present, place = around(direction)

        @pl.when(present)
        def _(place=place):
            pl.semaphore_signal(barrier, inc=1, device_id=place, device_id_type=MESH)

        expected = expected + present.astype(jnp.int32)
    return lambda: pl.semaphore_wait(barrier, expected)


def sent(direction, sizes):
    own, ext = [], []
    for step, size in zip(direction, sizes):
        own.append(pl.ds(0, size) if step == 0 else pl.ds(0 if step < 0 else size - 1, 1))
        ext.append(pl.ds(1, size) if step == 0 else pl.ds(size + 1 if step < 0 else 0, 1))
    return tuple(own), tuple(ext)


def rim(direction, sizes):
    return tuple(
        pl.ds(1, size) if step == 0 else pl.ds(0 if step < 0 else size + 1, 1)
        for step, size in zip(direction, sizes)
    )


def exchange(pairs, send_sem, recv_sem):
    copies = []
    for at, (direction, (source, target)) in enumerate(zip(DIRECTIONS, pairs)):
        present, place = around(direction)
        copy = pltpu.make_async_remote_copy(
            src_ref=source,
            dst_ref=target,
            send_sem=send_sem.at[at],
            recv_sem=recv_sem.at[at],
            device_id=place,
            device_id_type=MESH,
        )
        pl.when(present)(copy.start)
        copies.append((copy, present, around(opposite(direction))[0]))

    def finish():
        for copy, _, arrives in copies:
            pl.when(arrives)(copy.wait_recv)
        for copy, present, _ in copies:
            pl.when(present)(copy.wait_send)

    return finish


def blank_rim(ext, sizes):
    for direction in DIRECTIONS:

        @pl.when(jnp.logical_not(around(direction)[0]))
        def _(direction=direction):
            index = rim(direction, sizes)
            ext[index] = jnp.zeros(tuple(part.size for part in index) + ext.shape[3:], ext.dtype)


def spread_rim(own, ext, sizes, send_sem, recv_sem):
    pairs = []
    for direction in DIRECTIONS:
        mine, theirs = sent(direction, sizes)
        pairs.append((own.at[mine], ext.at[theirs]))
    return exchange(pairs, send_sem, recv_sem)


def halo_kernel(own, ext, send_sem, recv_sem, copy_sem):
    ready = greet()
    sizes = own.shape[:3]
    fill = pltpu.make_async_copy(own, ext.at[tuple(pl.ds(1, size) for size in sizes)], copy_sem)
    fill.start()
    blank_rim(ext, sizes)
    ready()
    finish = spread_rim(own, ext, sizes, send_sem, recv_sem)
    fill.wait()
    finish()


def start_kernel(positions, species, ext, send_sem, recv_sem, copy_sem, fresh):
    sizes = fresh.shape[:3]
    for x, y, z in cells_of(sizes):
        rows = [positions[x, y, d, z : z + 1, :] for d in range(3)]
        fresh[x, y, z] = tile_of(rows + [species[x, y, z : z + 1, :].astype(f32)])
    halo_kernel(fresh, ext, send_sem, recv_sem, copy_sem)


def tile_of(rows):
    row = lax.broadcasted_iota(jnp.int32, (8, rows[0].shape[-1]), 0)
    tile = jnp.zeros(row.shape, f32)
    for at, value in enumerate(rows):
        tile = jnp.where(row == at, value, tile)
    return tile


def mass_of(species, masses):
    mass = jnp.full(species.shape, masses[0], f32)
    for kind in range(1, masses.shape[0]):
        mass = jnp.where(species == kind, masses[kind], mass)
    return mass


def landing_scratch(sizes, tail, dtype):
    return [
        pltpu.VMEM(tuple(1 if step else size for step, size in zip(direction, sizes)) + tail, dtype)
        for direction in DIRECTIONS
    ]


def blank_lands(lands):
    for direction, land in zip(DIRECTIONS, lands):

        @pl.when(jnp.logical_not(around(opposite(direction))[0]))
        def _(land=land):
            land[...] = jnp.zeros_like(land)


def gather_rim(ext, lands, sizes, send_sem, recv_sem):
    pairs = [(ext.at[rim(direction, sizes)], land) for direction, land in zip(DIRECTIONS, lands)]
    return exchange(pairs, send_sem, recv_sem)


def cells_of(sizes):
    return [(x, y, z) for x in range(sizes[0]) for y in range(sizes[1]) for z in range(sizes[2])]


def landed(ext, lands, sizes, cell):
    value = ext[tuple(at + 1 for at in cell)].astype(f32)
    for direction, land in zip(DIRECTIONS, lands):
        index = []
        for step, size, at in zip(direction, sizes, cell):
            if step == 0:
                index.append(at)
            elif at == (size - 1 if step < 0 else 0):
                index.append(0)
        if len(index) == 3:
            value = value + land[tuple(index)].astype(f32)
    return value


def fold_kernel(ext, own, *refs):
    lands, (send_sem, recv_sem) = refs[:26], refs[26:]
    ready = greet()
    sizes = own.shape[:3]
    blank_lands(lands)
    ready()
    gather_rim(ext, lands, sizes, send_sem, recv_sem)()
    for cell in cells_of(sizes):
        own[cell] = landed(ext, lands, sizes, cell).astype(own.dtype)


def kick_kernel(masses, ext, positions, velocities, species, out_half, out_moved, out_pos, *refs):
    lands, (send_sem, recv_sem, send_two, recv_two, copy_sem, fresh) = refs[:26], refs[26:]
    ready = greet()
    sizes = fresh.shape[:3]
    blank_lands(lands)
    blank_rim(out_pos, sizes)
    ready()
    gather_rim(ext, lands, sizes, send_sem, recv_sem)()
    for cell in cells_of(sizes):
        x, y, z = cell
        kinds = species[x, y, z : z + 1, :]
        force = -landed(ext, lands, sizes, cell) * (0.5 * time_step / mass_of(kinds, masses))
        rows = []
        for d in range(3):
            half_kick = velocities[x, y, d, z : z + 1, :] + force[d : d + 1, :]
            moved = time_step * half_kick
            out_half[x, y, d, z : z + 1, :] = half_kick
            out_moved[x, y, d, z : z + 1, :] = moved
            rows.append(positions[x, y, d, z : z + 1, :] + moved)
        fresh[cell] = tile_of(rows + [kinds.astype(f32)])
    fill = pltpu.make_async_copy(fresh, out_pos.at[tuple(pl.ds(1, size) for size in sizes)], copy_sem)
    fill.start()
    finish = spread_rim(fresh, out_pos, sizes, send_two, recv_two)
    fill.wait()
    finish()


def ring(axes):
    steps = [()]
    for axis in axes:
        steps = [step + (t,) for step in steps for t in range(lax.axis_size(axis))]
    places = []
    for step in steps[1:]:
        places.append(
            {axis: lax.rem(lax.axis_index(axis) + t, lax.axis_size(axis)) for axis, t in zip(axes, step) if t}
        )
    return places


STAGES = (("gx", "gy"), ("gz",))


def last_kernel(slot_total, masses, ext, half, species, out, *refs):
    lands, refs = refs[:26], refs[26:]
    send_sem, recv_sem, send_two, recv_two, speed = refs[:5]
    inbox, sums = refs[5:7], refs[7:9]
    ready = greet([place for axes in STAGES for place in ring(axes)])
    sizes = speed.shape[:3]
    blank_lands(lands)
    ready()
    gather_rim(ext, lands, sizes, send_sem, recv_sem)()
    total = jnp.zeros(speed.shape[3:], f32)
    for cell in cells_of(sizes):
        x, y, z = cell
        kinds = species[x, y, z : z + 1, :]
        mass = mass_of(kinds, masses)
        force = -landed(ext, lands, sizes, cell) * (0.5 * time_step / mass)
        velocity = tile_of([half[x, y, d, z : z + 1, :] + force[d : d + 1, :] for d in range(3)])
        speed[cell] = velocity
        total = total + jnp.where(kinds > 0, 0.5 * mass, 0.0) * velocity * velocity
    base = 0
    for stage, axes in enumerate(STAGES):
        sums[stage][...] = total
        copies = []
        for t, place in enumerate(ring(axes)):
            copy = pltpu.make_async_remote_copy(
                src_ref=sums[stage],
                dst_ref=inbox[stage].at[t],
                send_sem=send_two.at[base],
                recv_sem=recv_two.at[base],
                device_id=place,
                device_id_type=MESH,
            )
            copy.start()
            copies.append(copy)
            base += 1
        for t, copy in enumerate(copies):
            copy.wait()
            total = total + inbox[stage][t]
    kinetic = jnp.sum(total, keepdims=True)
    factor = jnp.sqrt(target_slot * slot_total / (kinetic + tiny_eps))
    for x, y, z in cells_of(sizes):
        value = speed[x, y, z] * factor
        for d in range(3):
            out[x, y, d, z : z + 1, :] = value[d : d + 1, :]


def vmem_specs(count):
    return [pl.BlockSpec(memory_space=pltpu.VMEM)] * count


def remote_call(kernel, outs, scratch, collective_id, args, smem=()):
    return pl.pallas_call(
        kernel,
        out_shape=outs,
        in_specs=[pl.BlockSpec(memory_space=pltpu.SMEM)] * len(smem) + vmem_specs(len(args)),
        out_specs=vmem_specs(len(outs)),
        scratch_shapes=scratch,
        compiler_params=pltpu.CompilerParams(
            collective_id=collective_id, has_side_effects=True, vmem_limit_bytes=5 << 20
        ),
    )(*smem, *args)


def semaphores():
    return [pltpu.SemaphoreType.DMA((26,)), pltpu.SemaphoreType.DMA((26,))]


def padded_shape(shape, dtype):
    return jax.ShapeDtypeStruct(tuple(size + 2 for size in shape[:3]) + shape[3:], dtype)


def padded(cells, collective_id):
    scratch = semaphores() + [pltpu.SemaphoreType.DMA]
    return remote_call(halo_kernel, [padded_shape(cells.shape, cells.dtype)], scratch, collective_id, (cells,))[0]


def tiles_shape(species):
    return species.shape[:3] + (8,) + species.shape[3:]


def started(positions, species, collective_id):
    tiles = tiles_shape(species)
    scratch = semaphores() + [pltpu.SemaphoreType.DMA, pltpu.VMEM(tiles, f32)]
    return remote_call(start_kernel, [padded_shape(tiles, f32)], scratch, collective_id, (positions, species))[0]


def folded(grid, sizes, collective_id):
    tail = grid.shape[3:]
    scratch = landing_scratch(sizes, tail, grid.dtype) + semaphores()
    out = jax.ShapeDtypeStruct(sizes + tail, grid.dtype)
    return remote_call(fold_kernel, [out], scratch, collective_id, (grid,))[0]


def kicked(grid, positions, velocities, species, masses, collective_id):
    tiles = tiles_shape(species)
    scratch = landing_scratch(tiles[:3], tiles[3:], f32) + semaphores() + semaphores()
    scratch += [pltpu.SemaphoreType.DMA, pltpu.VMEM(tiles, f32)]
    raw = jax.ShapeDtypeStruct(positions.shape, f32)
    outs = [raw, raw, padded_shape(tiles, f32)]
    return remote_call(kick_kernel, outs, scratch, collective_id, (grid, positions, velocities, species), (masses,))


def thermostat(grid, half, species, masses, slot_total, collective_id):
    tiles = tiles_shape(species)
    counts = [math.prod(lax.axis_size(axis) for axis in axes) for axes in STAGES]
    peers = sum(count - 1 for count in counts)
    scratch = landing_scratch(tiles[:3], tiles[3:], f32) + semaphores()
    scratch += [pltpu.SemaphoreType.DMA((peers,)), pltpu.SemaphoreType.DMA((peers,)), pltpu.VMEM(tiles, f32)]
    scratch += [pltpu.VMEM((max(count - 1, 1),) + tiles[3:], f32) for count in counts]
    scratch += [pltpu.VMEM(tiles[3:], f32)] * 2
    out = jax.ShapeDtypeStruct(half.shape, f32)
    kernel = functools.partial(last_kernel, float(slot_total))
    return remote_call(kernel, [out], scratch, collective_id, (grid, half, species), (masses,))[0]


def slot_tables(neighbour_blocks):
    size_x, size_y, size_z, slot_count = neighbour_blocks.shape
    is_live = neighbour_blocks < 27
    offset = jnp.where(is_live, neighbour_blocks, 13)
    index_x = lax.broadcasted_iota(jnp.int32, neighbour_blocks.shape, 0)
    index_y = lax.broadcasted_iota(jnp.int32, neighbour_blocks.shape, 1)
    index_z = lax.broadcasted_iota(jnp.int32, neighbour_blocks.shape, 2)
    source = (
        (index_x + offset // 9) * (size_y + 2) + (index_y + offset // 3 % 3)
    ) * (size_z + 2) + (index_z + offset % 3)
    return source.reshape(-1, slot_count)


def basis_constants(basis_count):
    step = 5.0 / basis_count
    mid = basis_count // 2
    centers = [(k + 0.5) * step for k in range(basis_count)]
    scales = [math.exp(-gamma_width * (centers[k] - centers[mid]) ** 2) for k in range(basis_count)]
    return step, mid, centers, scales


def geometry(apart, row0, basis_count):
    step, mid, centers, _ = basis_constants(basis_count)
    atoms = apart.shape[1] // 3
    rows = slice(row0, row0 + CHUNK)
    steps = [apart[rows, d * atoms : (d + 1) * atoms] for d in range(3)]
    dx, dy, dz = steps
    squared = jnp.minimum(dx * dx + dy * dy + dz * dz, cut_sq)
    cut = 1.0 - squared * (1.0 / cut_sq)
    soft = squared + soft_sq
    inv = lax.rsqrt(soft)
    shift = soft * inv - centers[mid]
    bell = jnp.exp2((-gamma_width * LOG2E) * (shift * shift))
    slope = shift * (2.0 * gamma_width * step * LOG2E)
    return steps, cut, inv, bell, jnp.exp2(slope), jnp.exp2(-slope)


def radial_powers(start, up, down, basis_count):
    mid = basis_count // 2
    powers = [None] * basis_count
    powers[mid] = start
    for k in range(mid + 1, basis_count):
        powers[k] = powers[k - 1] * up
    for k in range(mid - 1, -1, -1):
        powers[k] = powers[k + 1] * down
    scales = basis_constants(basis_count)[3]
    return [power * scale if scale != 1.0 else power for power, scale in zip(powers, scales)]


def fill_kernel(store, apart, c, basis_count):
    rows, atoms = apart.shape[0], apart.shape[1] // 3
    for row0 in range(0, rows, CHUNK):
        _, cut, _, bell, up, down = geometry(apart, row0, basis_count)
        ahead = lax.broadcasted_iota(jnp.int32, cut.shape, 1) - lax.broadcasted_iota(jnp.int32, cut.shape, 0)
        cut = jnp.where(ahead == row0 + c * rows, 0.0, cut)
        for k, value in enumerate(radial_powers(cut * cut * bell, up, down, basis_count)):
            store[row0 : row0 + CHUNK, k * atoms : (k + 1) * atoms] = value.astype(bf16)


def split(value):
    high = value.astype(bf16)
    return high, (value - high.astype(f32)).astype(bf16)


def dot_split(a, value):
    high, low = split(value)
    return dot(a, high) + dot(a, low)


def held(value):
    return value.astype(bf16).astype(f32)


def narrowed(radial, sums):
    atoms = radial[0].shape[-1]
    return sum(column * sums[:, k * atoms : (k + 1) * atoms] for k, column in enumerate(radial))


def silu_grad(value):
    gate = jax.nn.sigmoid(value)
    return gate * (1.0 + value * (1.0 - gate))


def dot(a, b):
    return jnp.dot(a, b, preferred_element_type=f32)


def dot_wide(a, b):
    return jnp.dot(a, b, preferred_element_type=f32, precision=lax.Precision.HIGHEST)


def dot_nt(a, b):
    return lax.dot_general(a, b, (((1,), (1,)), ((), ())), preferred_element_type=f32)


def dot_tn(a, b):
    return lax.dot_general(a, b, (((0,), (0,)), ((), ())), preferred_element_type=f32)


FEATS = 32


def thirds(value):
    high = held(value)
    rest = value - high
    mid = held(rest)
    return high, mid, rest - mid


def side(values):
    return jnp.concatenate(values, axis=1)


def features(block, origin):
    row = lax.broadcasted_iota(jnp.int32, block.shape, 0)
    where = jnp.where(row < 3, block - origin, 0.0)
    square = jnp.sum(where * where, axis=0, keepdims=True) * near_part
    high = held(square)
    tiles = [jnp.where(row < 3, part, jnp.where(row == 3, 1.0, 0.0)) for part in thirds(where)]
    again = pltpu.roll(jnp.where(row < 3, tiles[0], 0.0), 4, 0)
    kinds = jnp.where((row > 3) & (block[3:4, :] == row.astype(f32) - 4.0), 1.0, 0.0)
    tiles[0] = jnp.where(row > 3, kinds, tiles[0])
    tiles[1] = jnp.where(row == 4, high, jnp.where(row == 5, square - high, tiles[1]))
    tiles[2] = tiles[2] + again
    return jnp.concatenate(tiles + [kinds], axis=0).astype(bf16)


near_part = 1.0 - 2.0**-13


def reach_rows(own, origin):
    row = lax.broadcasted_iota(jnp.int32, own.shape, 0)
    where = jnp.where(row < 3, own - origin, 0.0)
    square = jnp.sum(where * where, axis=0, keepdims=True) * near_part
    square = jnp.where(own[3:4, :] > 0.0, square, 1e9)
    top = held(square)
    high, mid, _ = thirds(where)
    tiles = [
        jnp.where(row == 3, top, -2.0 * high),
        jnp.where(row == 3, square - top, jnp.where((row == 4) | (row == 5), 1.0, -2.0 * high)),
        pltpu.roll(-2.0 * mid, 4, 0),
        jnp.zeros_like(own),
    ]
    return jnp.concatenate(tiles, axis=0).astype(bf16)


def set_apart(rel, own, origin):
    atoms = own.shape[-1]
    row = lax.broadcasted_iota(jnp.int32, (FEATS, atoms), 0)
    high, mid, low = thirds(own - origin)
    for d in range(3):
        tile = jnp.where((row == d) | (row == 8 + d) | (row == 16 + d), 1.0, 0.0)
        for at, part in ((3, high), (11, mid), (19, low)):
            tile = jnp.where(row == at, -part[d : d + 1, :], tile)
        rel[:, d * atoms : (d + 1) * atoms] = tile.astype(bf16)


def list_kernel(home, src, pos, dest, count, table, rel, hits):
    blocks, slots = src.shape
    atoms = pos.shape[-1]
    origin = pos[home[0]][:, 0:1]
    for b in range(blocks):
        own = pos[home[b]]
        set_apart(rel.at[b], own, origin)
        for q in range(slots):
            table[b, :, q * atoms : (q + 1) * atoms] = features(pos[src[b, q]], origin)
    for b in range(blocks):
        reach = dot_tn(reach_rows(pos[home[b]], origin), table[b])
        reach = jnp.min(reach, axis=0, keepdims=True)
        for q in range(slots):
            live = 1.0 if q == 0 else (src[b, q] != home[b]).astype(f32)
            real = pos[src[b, q]][3:4, :] > 0.0
            near = (reach[:, q * atoms : (q + 1) * atoms] < cut_sq * 1.001) & real
            hits[b * slots + q : b * slots + q + 1, :] = jnp.where(near, live, 0.0)
    hit = hits[...]
    shape = (atoms, atoms)
    upto = lax.broadcasted_iota(jnp.int32, shape, 0) <= lax.broadcasted_iota(jnp.int32, shape, 1)
    inside = dot(hit.astype(bf16), jnp.where(upto, 1.0, 0.0).astype(bf16))
    total = jnp.broadcast_to(inside[:, atoms - 1 : atoms], hit.shape)
    pairs = blocks * slots
    r0 = lax.broadcasted_iota(jnp.int32, (pairs, pairs), 0)
    r1 = lax.broadcasted_iota(jnp.int32, (pairs, pairs), 1)
    group0 = jnp.floor((r0.astype(f32) + 0.5) * (1.0 / slots))
    group1 = jnp.floor((r1.astype(f32) + 0.5) * (1.0 / slots))
    before = jnp.where((group0 == group1) & (r1 < r0), 1.0, 0.0).astype(bf16)
    start = dot(before, total.astype(bf16))
    dest[...] = jnp.where(hit > 0.0, start + inside - 1.0, -1.0).astype(jnp.int32)
    line = lax.broadcasted_iota(jnp.int32, hit.shape, 0)
    lane = lax.broadcasted_iota(jnp.int32, hit.shape, 1)
    last = jnp.where(line == lane * slots + (slots - 1), start + total, 0.0)
    count[...] = jnp.sum(last, axis=0, keepdims=True).astype(jnp.int32)


def set_places(place, dest, b, c):
    rows, atoms = place.shape[0], dest.shape[1]
    slots = place.shape[1] // atoms
    to = dest[pl.ds(pl.multiple_of(b * slots, slots), slots), :]
    to = jnp.clip(to - c * rows, -1, rows).astype(f32)
    row = lax.broadcasted_iota(jnp.int32, (rows, atoms), 0).astype(f32).astype(bf16)
    one, none = jnp.ones((rows, atoms), bf16), jnp.zeros((rows, atoms), bf16)
    for q in range(slots):
        here = jnp.broadcast_to(to[q : q + 1, :], (rows, atoms)).astype(bf16)
        place[:, q * atoms : (q + 1) * atoms] = jnp.where(here == row, one, none)


def plan(count, plan_ref, blocks, rows):
    def of_block(b, n):
        chunks = jnp.maximum(count[0, b] + (rows - 1), rows) // rows

        def of_chunk(c, n):
            plan_ref[0, n] = b
            plan_ref[1, n] = c
            return n + 1

        return lax.fori_loop(0, chunks, of_chunk, n)

    return lax.fori_loop(0, blocks, of_block, 0)


def pipelined(total, plan_ref, stages):
    last = len(stages) - 1

    def run(t, chosen):
        for s in reversed(chosen):
            n = t - s
            stages[s](n, plan_ref[0, n], plan_ref[1, n])

    def step(t, carry):
        run(t, range(last + 1))
        return carry

    for t in range(last):
        run(t, range(t + 1))
    lax.fori_loop(last, total, step, 0)
    for t in range(last):
        run(total + t, range(t + 1, last + 1))


def unpacked(pack, kinds):
    size = pack.shape[1]
    squares = [pack[at * size : (at + 1) * size, :] for at in range(5)]
    return squares[:2], squares[2:4], squares[4], pack[5 * size : 5 * size + kinds, :]


def mix_rows(embedding, w_send, w_radial):
    kinds, channels = embedding.shape
    rows = dot(embedding, w_send[0]).astype(bf16).astype(f32)
    row = lax.broadcasted_iota(jnp.int32, (8, channels), 0)
    tile = jnp.zeros((8, channels), f32)
    for kind in range(1, kinds):
        tile = jnp.where(row == 4 + kind, rows[kind : kind + 1, :], tile)
    return jnp.concatenate([tile * w_radial[0, k : k + 1, :] for k in range(w_radial.shape[1])], axis=0)


def columns(rows, atoms):
    turned = rows.T
    return [jnp.broadcast_to(turned[:, k : k + 1], (turned.shape[0], atoms)) for k in range(rows.shape[0])]


def first_kernel(home, kinds, src, count, pos, dest, table, rel, pack, w_radial,
                 h1_out, u1_out, s2_out, listed, place, apart, store, sums, stack, plan_ref):
    blocks, slots = src.shape
    atoms = pos.shape[-1]
    basis_count = store.shape[2] // atoms
    total = plan(count, plan_ref, blocks, store.shape[1])
    sums[...] = jnp.zeros_like(sums)

    def places(n, b, c):
        set_places(place.at[n & 1], dest, b, c)

    def gather(n, b, c):
        listed[n & 3] = dot_nt(place[n & 1], table[b]).astype(bf16)

    def differ(n, b, c):
        apart[n & 1] = dot(listed[n & 3], rel[b])

    def fill(n, b, c):
        fill_kernel(store.at[n & 1], apart.at[n & 1], c, basis_count)

    def collect(n, b, c):
        sums[b] += dot_tn(listed[n & 3][:, :8], store[n & 1])

    pipelined(total, plan_ref, [places, gather, differ, fill, collect])
    w_send, w_update, _, embedding = unpacked(pack, kinds)
    row = lax.broadcasted_iota(jnp.int32, (embedding.shape[0], atoms), 0).astype(f32)
    species = [pos[home[b]][3:4, :] for b in range(blocks)]
    onehot = side([jnp.where(row == one, 1.0, 0.0) for one in species]).astype(bf16)
    for b in range(blocks):
        for k in range(basis_count):
            stack[k * 8 : (k + 1) * 8, b * atoms : (b + 1) * atoms] = sums[b, :, k * atoms : (k + 1) * atoms]
    mix = mix_rows(embedding, w_send, w_radial)
    message = lax.dot_general(
        mix, stack[...], (((0,), (0,)), ((), ())), preferred_element_type=f32, precision=lax.Precision.HIGHEST
    )
    update = dot_tn(w_update[0], message.astype(bf16))
    hidden = (dot_tn(embedding, onehot) + update * jax.nn.sigmoid(update)).astype(bf16)
    sender = jnp.where(side(species) > 0.0, dot_tn(w_send[1], hidden), 0.0).astype(bf16)
    for b in range(blocks):
        there = slice(b * atoms, (b + 1) * atoms)
        h1_out[b] = hidden[:, there]
        u1_out[b] = update[:, there]
        s2_out[b] = sender[:, there]


def set_table(full, table, s2, src):
    blocks, slots = src.shape
    atoms = s2.shape[2]
    channels = s2.shape[1]
    full[:, channels:, :] = table[...]
    for b in range(blocks):
        for q in range(slots):
            full[b, :channels, q * atoms : (q + 1) * atoms] = s2[src[b, q]]


def second_kernel(home, src, count, pos, dest, table, rel, s2, h1, pack, w_radial,
                  energy, g2_out, dh2_out, ds_out, listed, wide_rel, full, place, apart, store, acc, sums, wide,
                  both, plan_ref):
    blocks, slots = src.shape
    channels, atoms = s2.shape[1:]
    basis_count = w_radial.shape[1]
    total = plan(count, plan_ref, blocks, store.shape[1])
    set_table(full, table, s2, src)
    wide_rel[:, :channels, :] = jnp.zeros((blocks, channels, rel.shape[2]), bf16)
    wide_rel[:, channels:, :] = rel[...]
    sums[...] = jnp.zeros_like(sums)

    def places(n, b, c):
        set_places(place.at[n & 1], dest, b, c)

    def gather(n, b, c):
        listed[n] = dot_nt(place[n & 1], full[b]).astype(bf16)

    def differ(n, b, c):
        apart[n & 1] = dot(listed[n], wide_rel[b])

    def fill(n, b, c):
        fill_kernel(store.at[n], apart.at[n & 1], c, basis_count)

    def collect(n, b, c):
        sums[b] += dot_tn(listed[n][:, :channels], store[n])

    pipelined(total, plan_ref, [places, gather, differ, fill, collect])
    _, w_update, w_out, _ = unpacked(pack, 1)
    radial = columns(w_radial[1], atoms)
    message = side([narrowed(radial, sums.at[b]) for b in range(blocks)])
    up = dot_tn(w_update[1], message.astype(bf16))
    second = side([h1[b] for b in range(blocks)]).astype(f32) + up * jax.nn.sigmoid(up)
    hidden = dot_tn(w_out, second.astype(bf16))
    real = side([pos[home[b]][3:4, :] for b in range(blocks)]) > 0.0
    d_hidden = jnp.where(real, columns(energy[...], blocks * atoms)[0] * silu_grad(hidden), 0.0)
    d_second = held(dot_split(w_out, d_hidden))
    g2 = dot_split(w_update[1], d_second * silu_grad(up)).astype(bf16)
    for b in range(blocks):
        there = slice(b * atoms, (b + 1) * atoms)
        dh2_out[b] = d_second[:, there]
        g2_out[b] = g2[:, there]
        turned = g2[:, there].astype(f32).T
        for k in range(basis_count):
            wide[b, k * atoms : (k + 1) * atoms, :] = (turned * w_radial[1, k : k + 1, :]).astype(bf16)
    sums[...] = jnp.zeros_like(sums)

    def project(n, b, c):
        both[n & 1] = dot(store[n], wide[b]).astype(bf16)
        set_places(place.at[n & 1], dest, b, c)

    def scatter(n, b, c):
        sums[b] += dot_tn(both[n & 1], place[n & 1])

    pipelined(total, plan_ref, [project, scatter])
    acc[...] = jnp.zeros_like(acc)
    for b in range(blocks):
        for q in range(slots):
            acc[src[b, q]] += sums[b, :, q * atoms : (q + 1) * atoms]
    ds_out[...] = acc[...].astype(bf16)


def third_kernel(home, kinds, src, count, pos, dest, rel, listed, g2, dh2, ds, u1, pack, w_radial,
                 grad_out, place, apart, wide, parts, pulls, turned, back, pull, plan_ref):
    blocks, slots = src.shape
    channels, atoms = g2.shape[1:]
    rows = parts.shape[1]
    basis_count = w_radial.shape[1]
    _, _, centers, _ = basis_constants(basis_count)
    total = plan(count, plan_ref, blocks, rows)
    row16 = lax.broadcasted_iota(jnp.int32, (16, rows), 0)
    unit = lax.broadcasted_iota(jnp.int32, (16, atoms), 0)
    folds = side([jnp.where((unit == d) | (unit == 8 + d), 1.0, 0.0) for d in range(3)]).astype(bf16)
    real = side([pos[home[b]][3:4, :] for b in range(blocks)]) > 0.0

    w_send, w_update, _, embedding = unpacked(pack, kinds)

    def joined(ref):
        return side([ref[b] for b in range(blocks)])

    dh1 = held(joined(dh2) + dot(w_send[1], joined(ds)))
    du1 = dh1 * silu_grad(joined(u1))
    g1 = jnp.where(real, dot_split(w_update[0], du1), 0.0)
    by_kind = dot_wide(mix_rows(embedding, w_send, w_radial), g1)
    radial = columns(w_radial[1], atoms)
    blank = jnp.zeros((FEATS - 16, atoms), f32)
    for b in range(blocks):
        g2_here = g2[b].astype(f32)
        for k in range(basis_count):
            there = slice(k * atoms, (k + 1) * atoms)
            first = by_kind[k * 8 : (k + 1) * 8, b * atoms : (b + 1) * atoms]
            high = held(first)
            wide[b, channels:, there] = jnp.concatenate([high, blank, first - high], axis=0).astype(bf16)
            wide[b, :channels, there] = (radial[k] * g2_here).astype(bf16)
    back[...] = jnp.zeros_like(back)
    pull[...] = jnp.zeros_like(pull)

    def differ(n, b, c):
        apart[n & 1] = dot(listed[n], rel[b])
        parts[n & 1] = dot(listed[n], wide[b])

    def pair(n, b, c):
        sides = [jnp.zeros((8, atoms), f32)] * 3
        for row0 in range(0, rows, CHUNK):
            steps, cut, inv, bell, up, down = geometry(apart.at[n & 1], row0, basis_count)
            plain = jnp.zeros_like(cut)
            moment = jnp.zeros_like(cut)
            for k, value in enumerate(radial_powers(bell, up, down, basis_count)):
                term = value * parts[n & 1, row0 : row0 + CHUNK, k * atoms : (k + 1) * atoms]
                plain = plain + term
                moment = moment + centers[k] * term
            scaled = gamma_width * cut
            size = cut * (moment * (scaled * inv) - plain * (scaled + 2.0 / cut_sq))
            for d in range(3):
                force = size * steps[d]
                pulls[n & 1, row0 : row0 + CHUNK, d * atoms : (d + 1) * atoms] = force.astype(bf16)
                sides[d] = sides[d] + jnp.sum(force.reshape(CHUNK // 8, 8, atoms), axis=0)
        pull[b] += jnp.concatenate(sides, axis=0)

    def turn(n, b, c):
        value = dot_nt(folds, pulls[n & 1])
        high = held(value)
        turned[n & 1] = jnp.where(row16 < 8, high, value - high).astype(bf16)
        set_places(place.at[n & 1], dest, b, c)

    def scatter(n, b, c):
        back[b] += dot(turned[n & 1], place[n & 1])

    pipelined(total, plan_ref, [differ, pair, turn, scatter])
    grad_out[...] = jnp.zeros_like(grad_out)
    row8 = lax.broadcasted_iota(jnp.int32, (8, atoms), 0)
    for b in range(blocks):
        for q in range(slots):
            there = slice(q * atoms, (q + 1) * atoms)
            grad_out[src[b, q]] += 2.0 * (back[b, :8, there] + back[b, 8:, there])
        for d in range(3):
            at_target = jnp.sum(pull[b, d * 8 : (d + 1) * 8, :], axis=0, keepdims=True)
            grad_out[home[b]] -= jnp.where(row8 == d, 2.0 * at_target, 0.0)


def call(kernel, outs, scratch, smem, args, limit):
    return pl.pallas_call(
        kernel,
        out_shape=outs,
        in_specs=[pl.BlockSpec(memory_space=pltpu.SMEM)] * len(smem)
        + [pl.BlockSpec(memory_space=pltpu.VMEM)] * len(args),
        out_specs=[pl.BlockSpec(memory_space=pltpu.VMEM)] * len(outs),
        scratch_shapes=scratch,
        compiler_params=pltpu.CompilerParams(vmem_limit_bytes=limit << 20),
    )(*smem, *args)


def local(
    positions,
    velocities,
    species,
    neighbour_blocks,
    embedding,
    w_send,
    w_radial,
    w_update,
    w_out,
    w_energy,
    masses,
):
    grid_x, grid_y, grid_z = positions.shape[:3]
    atoms = positions.shape[-1]
    channels = w_send.shape[-1]
    basis_count = w_radial.shape[1]
    kinds = masses.shape[0]
    blocks = grid_x * grid_y * grid_z
    ext_shape = (grid_x + 2, grid_y + 2, grid_z + 2)
    ext_count = ext_shape[0] * ext_shape[1] * ext_shape[2]
    home = [
        ((x + 1) * ext_shape[1] + y + 1) * ext_shape[2] + z + 1
        for x in range(grid_x)
        for y in range(grid_y)
        for z in range(grid_z)
    ]
    src = slot_tables(neighbour_blocks)
    slots = src.shape[1]
    energy = w_energy[None, :]
    squares = [value.reshape(-1, channels) for value in (w_send, w_update, w_out)]
    pack = jnp.concatenate(squares + [jnp.pad(embedding, ((0, -kinds % 16), (0, 0)))])
    wide = basis_count * atoms
    spread = slots * atoms

    def shaped(count, dtype):
        return jax.ShapeDtypeStruct((count, channels, atoms), dtype)

    def grid_of(value):
        return value.reshape((grid_x, grid_y, grid_z) + value.shape[1:])

    def flat(value):
        return value.reshape((-1,) + value.shape[3:])

    def gradient(pos):
        dest, count, table, rel = call(
            functools.partial(list_kernel, home),
            [
                jax.ShapeDtypeStruct((blocks * slots, atoms), jnp.int32),
                jax.ShapeDtypeStruct((1, atoms), jnp.int32),
                jax.ShapeDtypeStruct((blocks, FEATS, spread), bf16),
                jax.ShapeDtypeStruct((blocks, FEATS, 3 * atoms), bf16),
            ],
            [pltpu.VMEM((blocks * slots, atoms), f32)],
            (src,),
            (pos,),
            4,
        )
        smem = (src, count)
        lists = (pos, dest, table, rel)
        rows = atoms + atoms // 4
        chunks = blocks * (-(-slots * atoms // rows))
        plan_ref = pltpu.SMEM((2, chunks), jnp.int32)
        h1, u1, s2_own = call(
            functools.partial(first_kernel, home, kinds),
            [shaped(blocks, bf16), shaped(blocks, f32), shaped(blocks, bf16)],
            [
                pltpu.VMEM((4, rows, FEATS), bf16),
                pltpu.VMEM((2, rows, spread), bf16),
                pltpu.VMEM((2, rows, 3 * atoms), f32),
                pltpu.VMEM((2, rows, wide), bf16),
                pltpu.VMEM((blocks, 8, wide), f32),
                pltpu.VMEM((basis_count * 8, blocks * atoms), f32),
                plan_ref,
            ],
            smem,
            lists + (pack, w_radial),
            7,
        )
        s2 = flat(padded(grid_of(s2_own), 1))
        g2, dh2, ds, listed, wide_rel = call(
            functools.partial(second_kernel, home),
            [
                shaped(blocks, bf16),
                shaped(blocks, f32),
                shaped(ext_count, bf16),
                jax.ShapeDtypeStruct((chunks, rows, FEATS + channels), bf16),
                jax.ShapeDtypeStruct((blocks, FEATS + channels, 3 * atoms), bf16),
            ],
            [
                pltpu.VMEM((blocks, FEATS + channels, spread), bf16),
                pltpu.VMEM((2, rows, spread), bf16),
                pltpu.VMEM((2, rows, 3 * atoms), f32),
                pltpu.VMEM((chunks, rows, wide), bf16),
                pltpu.VMEM((ext_count, channels, atoms), f32),
                pltpu.VMEM((blocks, channels, max(wide, spread)), f32),
                pltpu.VMEM((blocks, wide, channels), bf16),
                pltpu.VMEM((2, rows, channels), bf16),
                plan_ref,
            ],
            smem,
            lists + (s2, h1, pack, w_radial, energy),
            36,
        )
        ds_own = flat(folded(ds.reshape(ext_shape + ds.shape[1:]), (grid_x, grid_y, grid_z), 2))
        (grad,) = call(
            functools.partial(third_kernel, home, kinds),
            [jax.ShapeDtypeStruct((ext_count, 8, atoms), f32)],
            [
                pltpu.VMEM((2, rows, spread), bf16),
                pltpu.VMEM((2, rows, 3 * atoms), f32),
                pltpu.VMEM((blocks, FEATS + channels, wide), bf16),
                pltpu.VMEM((2, rows, wide), f32),
                pltpu.VMEM((2, rows, 3 * atoms), bf16),
                pltpu.VMEM((2, 16, rows), bf16),
                pltpu.VMEM((blocks, 16, spread), f32),
                pltpu.VMEM((blocks, 24, atoms), f32),
                plan_ref,
            ],
            smem,
            (pos, dest, wide_rel, listed, g2, dh2, ds_own, u1, pack, w_radial),
            11,
        )
        return grad.reshape(ext_shape + grad.shape[1:])

    def turned(value):
        return jnp.swapaxes(value, 2, 3)

    slot_total = (
        positions.size // 3 * lax.axis_size("gx") * lax.axis_size("gy") * lax.axis_size("gz")
    )
    positions, velocities = turned(positions), turned(velocities)
    pos = started(positions, species, 0)
    half, travelled, pos = kicked(gradient(flat(pos)), positions, velocities, species, masses, 3)
    speeds = thermostat(gradient(flat(pos)), half, species, masses, slot_total, 4)
    return (turned(travelled), turned(speeds))


def solution(mesh):
    placed = (
        P("gx", "gy", "gz", None, None),
        P("gx", "gy", "gz", None, None),
        P("gx", "gy", "gz", None),
        P("gx", "gy", "gz", None),
        P(),
        P(),
        P(),
        P(),
        P(),
        P(),
        P(),
    )
    return jax.shard_map(
        local,
        mesh=mesh,
        in_specs=placed,
        out_specs=(P("gx", "gy", "gz", None, None), P("gx", "gy", "gz", None, None)),
        check_vma=False,
    )
```
